128 devices in a mesh: grp: 8 (over y, core), dom: 16 (over z, x).
Axes of the slice: x: 4, y: 4, z: 4, core: 2. Of those that a mesh axis runs over, the one named last changes fastest.
Arguments:
- diag_blocks: bfloat16 [2048, 384, 384], P(('grp', 'dom')), may hold values from -0.3125 to 0.3125
- face_in: bfloat16 [4096, 384, 384], P(('grp', 'dom')), may hold values from -0.3125 to 0.3125
- face_cross: bfloat16 [2048, 384, 384], P(('grp', 'dom')), may hold values from -0.3125 to 0.3125
- metric: float32 [2048, 384], P(('grp', 'dom')), may hold values from 0.5 to 2
- source_in: int32 [4096], P(('grp', 'dom')), may hold values from 0 to 15
- source_cross: int32 [2048], P(('grp', 'dom')), may hold values from 0 to 15
- orient_in: int32 [4096], P(('grp', 'dom')), may hold values from 0 to 7
- orient_cross: int32 [2048], P(('grp', 'dom')), may hold values from 0 to 7
- peer_in: int32 [4096, 1], P(('grp', 'dom')), may hold values from 0 to 15; in each aligned block of 32 rows (0 to 31, 32 to 63, ...) at most 3 rows name the same one
- peer_cross: int32 [2048, 1], P(('grp', 'dom')), may hold values from 0 to 7; in each aligned block of 16 rows (0 to 15, 16 to 31, ...) at most 3 rows name the same one
- target_in: int32 [4096], P(('grp', 'dom')), may hold values from 0 to 47
- target_cross: int32 [2048], P(('grp', 'dom')), may hold values from 0 to 47
Outputs:
- coarse_diag: float32 [2048, 2304], P('grp')
- coarse_face: float32 [2048, 6912], P('grp')
The draws below stay inside these ranges and needn't reach their ends.
Inputs may be any that keep to these rules, and one draw needn't show every extreme that they name: `peer_in`: at most 3 records of one device name the same partition; on some device exactly 3 do. `peer_cross`: at most 3 records of one device name the same group; on some device exactly 3 do.
All inputs are finite; a program needn't handle non-finite values.
Results may differ from the reference program's by a relative error of at most 0.0052.
Values may be sent and summed in bfloat16 or wider, within the bound.
A program may use at most 128 MiB of HBM per device.

```python
import math
import jax
import jax.numpy as jnp
import numpy as np
from jax import lax

VARS = 6
NP = 384
NC = 48
E_DEV = 16
FI = 32
FX = 16
CI = 3
CX = 3
ELEMS = 2048
FACES_IN = 4096
FACES_X = 2048
N_GRP = 8
N_DOM = 16


def place_ends(entries, stream_key, smallest, top_value):
    longest = entries.shape.index(max(entries.shape))
    spots = []
    for shift in (0, 1):
        where = [jax.random.randint(jax.random.fold_in(stream_key, axis), (), 0, length) for axis, length in enumerate(entries.shape)]
        where[longest] = (where[longest] + shift) % entries.shape[longest]
        spots.append(tuple(where))
    return entries.at[spots[0]].set(smallest).at[spots[1]].set(top_value)


def steps_of(own_key, extent, shards, smallest, high):
    def one(dim, blocks):
        steps = jax.random.uniform(jax.random.fold_in(jax.random.fold_in(own_key, 6), dim), (blocks,), jnp.float32, smallest / len(shards), high / len(shards))
        return jnp.repeat(jnp.exp(steps), extent[dim] // blocks).reshape((-1,) + (1,) * (len(extent) - dim - 1))

    loudness = one(*shards[0])
    for cut in shards[1:]:
        loudness = loudness * one(*cut)
    return loudness


def routed_block(rng, own, number, rows, number_of, top, reach, lean):
    order = jax.random.permutation(rng, number_of)
    heavy_load, usual = shares(number_of, rows * top, reach, lean, True), shares(number_of, rows * top, reach, lean, False)
    places = jnp.arange(number_of)

    def named(tallies, turn):
        used = int((tallies > 0).sum())
        fixed = max(1, used // 4)
        shifted = fixed + (places - fixed + turn * (used - fixed)) % max(1, number_of - fixed)
        return jnp.zeros((number_of,), jnp.int32).at[order[jnp.where(places < fixed, places, shifted)]].set(jnp.asarray(tallies, jnp.int32))

    tallies = jnp.where(number % 4 == 0, named(heavy_load, number // 4), named(usual, number - number // 4 - 1))
    mixed = jax.random.permutation(jax.random.fold_in(own, 3), number_of)
    giver, taker = mixed[0:number_of // 2 * 2:2], mixed[1:number_of // 2 * 2:2]
    slack = jnp.minimum(tallies[giver] - 1, reach - tallies[taker]) // 2
    slack = jnp.where((giver == order[0]) | (taker == order[0]) | (tallies[taker] == 0), 0, jnp.maximum(slack, 0))
    shifted = jax.random.randint(jax.random.fold_in(own, 4), (number_of // 2,), 0, 1 << 20) % (slack + 1)
    tallies = tallies.at[giver].add(-shifted).at[taker].add(shifted)
    items = jnp.searchsorted(jnp.cumsum(tallies), jnp.arange(rows * top), side="right").astype(jnp.int32)
    grid = items.reshape(top, rows).T
    grid = grid[jax.random.permutation(jax.random.fold_in(own, 1), rows)]
    turn = jax.random.randint(jax.random.fold_in(own, 2), (rows, 1), 0, top)
    return jnp.take_along_axis(grid, (jnp.arange(top)[None, :] + turn) % top, axis=1)


def shares(amount, total, bound, slope, full):
    weights = [(1 << 20) // math.isqrt(standing ** slope) + 1 for standing in range(1, amount + 1)]
    largest = bound if full else min(bound, max(-(-total // amount), total * weights[0] // sum(weights)))
    least = 1 if total - largest >= amount - 1 else 0
    holding, surplus = [largest] + [least] * (amount - 1), total - largest - least * (amount - 1)
    while surplus > 0:
        movable = [i for i in range(1, amount) if holding[i] < largest] or [i for i in range(1, amount) if holding[i] < bound]
        whole, budget = sum([weights[i] for i in movable]), surplus
        for i in movable:
            extra = min(bound - holding[i], max(1, budget * weights[i] // whole), surplus)
            holding[i] = holding[i] + extra
            surplus = surplus - extra
    return np.array(holding)


def bell_draw(stream_key, shape, width, most, shards=(), kind=jnp.bfloat16):
    drawn = jax.random.normal(stream_key, shape, jnp.float32) * width
    if len(shards) > 0:
        drawn = steps_of(stream_key, shape, shards, -0.22, 0.18) * drawn
    return jnp.clip(drawn, min=-most, max=most).astype(kind)


def setup_inputs(seed: int = 0) -> dict:
    seeds = jax.random.split(jax.random.key(seed), 13)
    diag_blocks = bell_draw(seeds[0], (ELEMS, NP, NP), NP ** -0.5, 0.3125, ((0, 128),))
    face_in = bell_draw(seeds[1], (FACES_IN, NP, NP), NP ** -0.5, 0.3125, ((0, 128),))
    face_cross = bell_draw(seeds[2], (FACES_X, NP, NP), NP ** -0.5, 0.3125, ((0, 128),))
    metric = jnp.clip(jnp.exp(math.log(2.0) - 1.3862944 * jax.random.uniform(seeds[3], (ELEMS, NP), jnp.float32) ** steps_of(seeds[3], (ELEMS, NP), ((0, 128),), -0.2, 0.2)), 0.5, 2.0)
    source_in = place_ends(jax.random.randint(seeds[4], (FACES_IN,), 0, E_DEV), jax.random.fold_in(seeds[4], 1), 0, E_DEV - 1).astype(jnp.int32)
    source_cross = place_ends(jax.random.randint(seeds[5], (FACES_X,), 0, E_DEV), jax.random.fold_in(seeds[5], 1), 0, E_DEV - 1).astype(jnp.int32)
    orient_in = place_ends(jax.random.randint(seeds[6], (FACES_IN,), 0, 8), jax.random.fold_in(seeds[6], 1), 0, 7).astype(jnp.int32)
    orient_cross = place_ends(jax.random.randint(seeds[7], (FACES_X,), 0, 8), jax.random.fold_in(seeds[7], 1), 0, 7).astype(jnp.int32)
    peer_in_keys = jax.random.split(jax.random.fold_in(seeds[8], 1), FACES_IN // FI)
    peer_in_turns = jax.random.permutation(jax.random.fold_in(seeds[8], 3), FACES_IN // FI)
    peer_in = jax.vmap(lambda own, number: routed_block(jax.random.fold_in(seeds[8], 2), own, number, FI, N_DOM, 1, CI, 2))(peer_in_keys, peer_in_turns).reshape((FACES_IN, 1))
    peer_cross_keys = jax.random.split(jax.random.fold_in(seeds[9], 1), FACES_X // FX)
    peer_cross_turns = jax.random.permutation(jax.random.fold_in(seeds[9], 3), FACES_X // FX)
    peer_cross = jax.vmap(lambda own, number: routed_block(jax.random.fold_in(seeds[9], 2), own, number, FX, N_GRP, 1, CX, 2))(peer_cross_keys, peer_cross_turns).reshape((FACES_X, 1))
    target_in = place_ends(jax.random.randint(seeds[10], (FACES_IN,), 0, 3 * E_DEV), jax.random.fold_in(seeds[10], 1), 0, (3 * E_DEV) - 1).astype(jnp.int32)
    target_cross = place_ends(jax.random.randint(seeds[11], (FACES_X,), 0, 3 * E_DEV), jax.random.fold_in(seeds[11], 1), 0, (3 * E_DEV) - 1).astype(jnp.int32)
    return dict(diag_blocks=diag_blocks, face_in=face_in, face_cross=face_cross, metric=metric, source_in=source_in, source_cross=source_cross, orient_in=orient_in, orient_cross=orient_cross, peer_in=peer_in, peer_cross=peer_cross, target_in=target_in, target_cross=target_cross)


def corner_table():
    nodes = -1.0 + 2.0 * jnp.arange(4, dtype=jnp.float32) / 3.0
    basis = jnp.stack(((1.0 - nodes) / 2.0, (1.0 + nodes) / 2.0), axis=1)
    cube = jnp.einsum("ia,jb,kc->abcijk", basis, basis, basis).reshape(8, 64)
    return jnp.kron(jnp.eye(VARS, dtype=jnp.float32), cube)


def restrictor(weights, orient):
    table = corner_table()
    full = weights[:, None, :] * table[None]
    shaped = full.reshape(-1, NC, VARS, 4, 4, 4)
    bits = orient.reshape(-1, 1, 1, 1, 1, 1)
    shaped = jnp.where(bits % 2 == 1, jnp.flip(shaped, 3), shaped)
    shaped = jnp.where(bits // 2 % 2 == 1, jnp.flip(shaped, 4), shaped)
    shaped = jnp.where(bits // 4 % 2 == 1, jnp.flip(shaped, 5), shaped)
    return shaped.reshape(-1, NC, NP).astype(jnp.bfloat16)


def triple(blocks, column_side, row_side):
    def single(items):
        block, right, left = items
        product = jnp.dot(right, block.T, preferred_element_type=jnp.float32).astype(jnp.bfloat16)
        return jnp.dot(left, product.T, preferred_element_type=jnp.float32)
    return lax.map(single, (blocks, column_side, row_side))


def reference(diag_blocks, face_in, face_cross, metric, source_in, source_cross, orient_in, orient_cross, peer_in, peer_cross, target_in, target_cross):
    zeros_elem = jnp.zeros((ELEMS,), jnp.int32)
    diag_side = restrictor(metric, zeros_elem)
    coarse_diag = triple(diag_blocks, diag_side, diag_side).reshape(ELEMS, NC * NC)

    record_in = jnp.arange(FACES_IN, dtype=jnp.int32)
    device_in = record_in // FI
    column_in = device_in * E_DEV + source_in
    owner_in = (device_in // N_DOM) * N_DOM + peer_in[:, 0]
    row_in = owner_in * E_DEV + target_in // 3
    slot_in = row_in * 3 + target_in % 3
    terms_in = triple(face_in, restrictor(metric[column_in], orient_in), restrictor(metric[row_in], jnp.zeros((FACES_IN,), jnp.int32)))

    record_x = jnp.arange(FACES_X, dtype=jnp.int32)
    device_x = record_x // FX
    column_x = device_x * E_DEV + source_cross
    owner_x = peer_cross[:, 0] * N_DOM + device_x % N_DOM
    row_x = owner_x * E_DEV + target_cross // 3
    slot_x = row_x * 3 + target_cross % 3
    terms_x = triple(face_cross, restrictor(metric[column_x], orient_cross), restrictor(metric[row_x], jnp.zeros((FACES_X,), jnp.int32)))

    summed = jax.ops.segment_sum(terms_in.reshape(FACES_IN, NC * NC), slot_in, num_segments=ELEMS * 3)
    summed = summed + jax.ops.segment_sum(terms_x.reshape(FACES_X, NC * NC), slot_x, num_segments=ELEMS * 3)
    return coarse_diag, summed.reshape(ELEMS, 3 * NC * NC)
```

```python
import jax
import jax.numpy as jnp
from jax import lax
from jax.sharding import PartitionSpec as P

CROSS_CAP = 3


def corner_table(var_count):
    nodes = -1.0 + 2.0 * jnp.arange(4, dtype=jnp.float32) / 3.0
    basis = jnp.stack(((1.0 - nodes) / 2.0, (1.0 + nodes) / 2.0), axis=1)
    cube = jnp.einsum("ia,jb,kc->abcijk", basis, basis, basis).reshape(8, 64)
    return jnp.kron(jnp.eye(var_count, dtype=jnp.float32), cube)


def restrictor(weights, orient):
    var_count = weights.shape[1] // 64
    table = corner_table(var_count)
    full = weights[:, None, :] * table[None]
    shaped = full.reshape(weights.shape[0], var_count * 8, var_count, 4, 4, 4)
    bits = orient.reshape(-1, 1, 1, 1, 1, 1)
    shaped = jnp.where(bits % 2 == 1, jnp.flip(shaped, 3), shaped)
    shaped = jnp.where(bits // 2 % 2 == 1, jnp.flip(shaped, 4), shaped)
    shaped = jnp.where(bits // 4 % 2 == 1, jnp.flip(shaped, 5), shaped)
    return shaped.reshape(weights.shape[0], var_count * 8, var_count * 64).astype(jnp.bfloat16)


def plain_restrictor(weights):
    table = corner_table(weights.shape[1] // 64)
    return (weights[:, None, :] * table[None]).astype(jnp.bfloat16)


def pick_rows(index, table):
    picks = (index[:, None] == jnp.arange(table.shape[0], dtype=jnp.int32)[None, :]).astype(
        jnp.float32
    )
    return jnp.dot(picks, table, precision=lax.Precision.HIGHEST)


def one_sided(blocks, column_side):
    return jnp.einsum(
        "rcj,rij->rci", column_side, blocks, preferred_element_type=jnp.float32
    ).astype(jnp.bfloat16)


def coarse_terms(row_side, products):
    return jnp.einsum("rci,rdi->rcd", row_side, products, preferred_element_type=jnp.float32)


def id_row(values, width):
    flat = values.reshape(-1).astype(jnp.bfloat16)
    return jnp.pad(flat, (0, width - flat.shape[0]))[None, :]


def per_device(
    diag_blocks,
    face_in,
    face_cross,
    metric,
    source_in,
    source_cross,
    orient_in,
    orient_cross,
    peer_in,
    peer_cross,
    target_in,
    target_cross,
):
    elem_count = metric.shape[0]
    coarse_width = metric.shape[1] // 8
    square = coarse_width * coarse_width
    slots_dev = 3 * elem_count
    group_width = lax.axis_size("dom")
    group_count = lax.axis_size("grp")
    my_dom = lax.axis_index("dom")
    my_grp = lax.axis_index("grp")
    inner_count = face_in.shape[0]
    cross_count = face_cross.shape[0]

    metric_dom = lax.all_gather(metric, "dom", axis=0, tiled=True)
    metric_grp = lax.all_gather(metric, "grp", axis=0, tiled=True)

    diag_side = plain_restrictor(metric)
    diag_c = coarse_terms(diag_side, one_sided(diag_blocks, diag_side))
    diag_rows = diag_c.reshape(elem_count, square).astype(jnp.bfloat16)
    diag_all = lax.all_gather(diag_rows, "dom", axis=0, tiled=True)

    cross_y = one_sided(face_cross, restrictor(pick_rows(source_cross, metric), orient_cross))
    peer_x = peer_cross[:, 0]
    cross_row_side = plain_restrictor(
        pick_rows(peer_x * elem_count + target_cross // 3, metric_grp)
    )
    cross_c = coarse_terms(cross_row_side, cross_y).reshape(cross_count, square)
    cross_ids = jnp.stack((peer_x, target_cross), axis=1)
    cross_packet = jnp.concatenate(
        (cross_c.astype(jnp.bfloat16), id_row(cross_ids, square)), axis=0
    )
    cross_got = lax.all_gather(cross_packet, "grp", axis=0)
    got_rows = cross_got[:, :cross_count, :]
    got_ids = cross_got[:, cross_count, : 2 * cross_count].astype(jnp.int32)
    got_peer = got_ids[:, 0::2]
    got_target = got_ids[:, 1::2]
    match = got_peer == my_grp
    rank = jnp.cumsum(match.astype(jnp.int32), axis=1) - 1
    picks = match[:, None, :] & (
        rank[:, None, :] == jnp.arange(CROSS_CAP, dtype=jnp.int32)[None, :, None]
    )
    mine_rows = jnp.einsum(
        "skr,srq->skq", picks.astype(jnp.bfloat16), got_rows, preferred_element_type=jnp.float32
    ).astype(jnp.bfloat16).reshape(group_count * CROSS_CAP, square)
    mine_target = jnp.sum(jnp.where(picks, got_target[:, None, :], 0), axis=2)
    mine_slot = jnp.where(
        jnp.any(picks, axis=2), my_dom * slots_dev + mine_target, -1
    ).reshape(-1)

    inner_y = one_sided(face_in, restrictor(pick_rows(source_in, metric), orient_in))
    peer_i = peer_in[:, 0]
    inner_row_side = plain_restrictor(
        pick_rows(peer_i * elem_count + target_in // 3, metric_dom)
    )
    inner_c = coarse_terms(inner_row_side, inner_y).reshape(inner_count, square)
    inner_slot = peer_i * slots_dev + target_in

    slots = jnp.concatenate((inner_slot, mine_slot), axis=0)
    valid = slots >= 0
    slot_code = jnp.stack(
        (jnp.where(valid, slots // 32, -1), jnp.where(valid, slots % 32, 0)), axis=1
    )
    face_packet = jnp.concatenate(
        (inner_c.astype(jnp.bfloat16), mine_rows, id_row(slot_code, square)), axis=0
    )
    face_all = lax.all_gather(face_packet, "dom", axis=0)
    contrib_count = slots.shape[0]
    contrib = face_all[:, :contrib_count, :].reshape(group_width * contrib_count, square)
    codes = face_all[:, contrib_count, : 2 * contrib_count].astype(jnp.int32)
    hi = codes[:, 0::2].reshape(-1)
    lo = codes[:, 1::2].reshape(-1)
    got_slot = jnp.where(hi >= 0, hi * 32 + lo, -1)
    group_slots = group_width * slots_dev
    onehot = (
        jnp.arange(group_slots, dtype=jnp.int32)[:, None] == got_slot[None, :]
    ).astype(jnp.bfloat16)
    face = jnp.dot(onehot, contrib, preferred_element_type=jnp.float32)

    coarse_diag = diag_all.astype(jnp.float32)
    coarse_face = face.reshape(group_width * elem_count, 3 * square)
    return (coarse_diag, coarse_face)


def solution(mesh):
    placed = (
        P(("grp", "dom"), None, None),
        P(("grp", "dom"), None, None),
        P(("grp", "dom"), None, None),
        P(("grp", "dom"), None),
        P(("grp", "dom")),
        P(("grp", "dom")),
        P(("grp", "dom")),
        P(("grp", "dom")),
        P(("grp", "dom"), None),
        P(("grp", "dom"), None),
        P(("grp", "dom")),
        P(("grp", "dom")),
    )
    return jax.shard_map(
        per_device,
        mesh=mesh,
        in_specs=placed,
        out_specs=(P("grp", None), P("grp", None)),
        check_vma=False,
    )
```

```python
import jax
import jax.numpy as jnp
from jax import lax
from jax.sharding import PartitionSpec as P
from jax.experimental import pallas as pl
from jax.experimental.pallas import tpu as pltpu

CROSS_CAP = 3


def corner_table(var_count):
    nodes = -1.0 + 2.0 * jnp.arange(4, dtype=jnp.float32) / 3.0
    basis = jnp.stack(((1.0 - nodes) / 2.0, (1.0 + nodes) / 2.0), axis=1)
    cube = jnp.einsum("ia,jb,kc->abcijk", basis, basis, basis).reshape(8, 64)
    return jnp.kron(jnp.eye(var_count, dtype=jnp.float32), cube)


def restrictor(weights, orient):
    var_count = weights.shape[1] // 64
    table = corner_table(var_count)
    full = weights[:, None, :] * table[None]
    shaped = full.reshape(weights.shape[0], var_count * 8, var_count, 4, 4, 4)
    bits = orient.reshape(-1, 1, 1, 1, 1, 1)
    shaped = jnp.where(bits % 2 == 1, jnp.flip(shaped, 3), shaped)
    shaped = jnp.where(bits // 2 % 2 == 1, jnp.flip(shaped, 4), shaped)
    shaped = jnp.where(bits // 4 % 2 == 1, jnp.flip(shaped, 5), shaped)
    return shaped.reshape(weights.shape[0], var_count * 8, var_count * 64).astype(jnp.bfloat16)


def plain_restrictor(weights):
    table = corner_table(weights.shape[1] // 64)
    return (weights[:, None, :] * table[None]).astype(jnp.bfloat16)


def pick_rows(index, table):
    picks = (index[:, None] == jnp.arange(table.shape[0], dtype=jnp.int32)[None, :]).astype(
        jnp.float32
    )
    return jnp.dot(picks, table, precision=lax.Precision.HIGHEST)


def one_sided(blocks, column_side):
    return jnp.einsum(
        "rcj,rij->rci", column_side, blocks, preferred_element_type=jnp.float32
    ).astype(jnp.bfloat16)


def coarse_terms(row_side, products):
    return jnp.einsum("rci,rdi->rcd", row_side, products, preferred_element_type=jnp.float32)


def direct_gather(x, axis, other, order, collective_id):
    n = lax.axis_size(axis)

    def device(peer):
        here = {axis: peer, other: lax.axis_index(other)}
        return tuple(here[name] for name in order)

    def kernel(x_ref, o_ref, send_sem, recv_sem, local_sem):
        me = lax.axis_index(axis)
        barrier = pltpu.get_barrier_semaphore()
        for step in range(1, n):
            pl.semaphore_signal(
                barrier, 1, device_id=device(lax.rem(me + step, n)),
                device_id_type=pl.DeviceIdType.MESH,
            )
        pl.semaphore_wait(barrier, n - 1)
        local = pltpu.make_async_copy(x_ref, o_ref.at[me], local_sem)
        local.start()
        sends = []
        for step in range(1, n):
            copy = pltpu.make_async_remote_copy(
                src_ref=x_ref,
                dst_ref=o_ref.at[me],
                send_sem=send_sem.at[step],
                recv_sem=recv_sem.at[step],
                device_id=device(lax.rem(me + step, n)),
                device_id_type=pl.DeviceIdType.MESH,
            )
            copy.start()
            sends.append(copy)
        for copy in sends:
            copy.wait_send()
        for step in range(1, n):
            source = lax.rem(me - step + n, n)
            pltpu.make_async_remote_copy(
                src_ref=x_ref,
                dst_ref=o_ref.at[source],
                send_sem=send_sem.at[step],
                recv_sem=recv_sem.at[step],
                device_id=device(source),
                device_id_type=pl.DeviceIdType.MESH,
            ).wait_recv()
        local.wait()

    return pl.pallas_call(
        kernel,
        out_shape=jax.ShapeDtypeStruct((n,) + x.shape, x.dtype),
        in_specs=[pl.BlockSpec(memory_space=pl.ANY)],
        out_specs=pl.BlockSpec(memory_space=pl.ANY),
        scratch_shapes=[
            pltpu.SemaphoreType.DMA((n,)),
            pltpu.SemaphoreType.DMA((n,)),
            pltpu.SemaphoreType.DMA,
        ],
        compiler_params=pltpu.CompilerParams(
            collective_id=collective_id, has_side_effects=True
        ),
    )(x)


def id_row(values, width):
    flat = values.reshape(-1).astype(jnp.bfloat16)
    return jnp.pad(flat, (0, width - flat.shape[0]))[None, :]


def per_device(
    diag_blocks,
    face_in,
    face_cross,
    metric,
    source_in,
    source_cross,
    orient_in,
    orient_cross,
    peer_in,
    peer_cross,
    target_in,
    target_cross,
):
    elem_count = metric.shape[0]
    coarse_width = metric.shape[1] // 8
    square = coarse_width * coarse_width
    slots_dev = 3 * elem_count
    group_width = lax.axis_size("dom")
    group_count = lax.axis_size("grp")
    my_dom = lax.axis_index("dom")
    my_grp = lax.axis_index("grp")
    inner_count = face_in.shape[0]
    cross_count = face_cross.shape[0]

    order = ("grp", "dom")
    metric_dom = direct_gather(metric, "dom", "grp", order, 0).reshape(-1, metric.shape[1])
    metric_grp = direct_gather(metric, "grp", "dom", order, 1).reshape(-1, metric.shape[1])

    diag_side = plain_restrictor(metric)
    diag_c = coarse_terms(diag_side, one_sided(diag_blocks, diag_side))
    diag_rows = diag_c.reshape(elem_count, square).astype(jnp.bfloat16)
    diag_all = lax.all_gather(diag_rows, "dom", axis=0, tiled=True)

    cross_y = one_sided(face_cross, restrictor(pick_rows(source_cross, metric), orient_cross))
    peer_x = peer_cross[:, 0]
    cross_row_side = plain_restrictor(
        pick_rows(peer_x * elem_count + target_cross // 3, metric_grp)
    )
    cross_c = coarse_terms(cross_row_side, cross_y).reshape(cross_count, square)
    cross_ids = jnp.stack((peer_x, target_cross), axis=1)
    cross_packet = jnp.concatenate(
        (cross_c.astype(jnp.bfloat16), id_row(cross_ids, square)), axis=0
    )
    cross_got = direct_gather(cross_packet, "grp", "dom", order, 2)
    got_rows = cross_got[:, :cross_count, :]
    got_ids = cross_got[:, cross_count, : 2 * cross_count].astype(jnp.int32)
    got_peer = got_ids[:, 0::2]
    got_target = got_ids[:, 1::2]
    match = got_peer == my_grp
    rank = jnp.cumsum(match.astype(jnp.int32), axis=1) - 1
    picks = match[:, None, :] & (
        rank[:, None, :] == jnp.arange(CROSS_CAP, dtype=jnp.int32)[None, :, None]
    )
    mine_rows = jnp.einsum(
        "skr,srq->skq", picks.astype(jnp.bfloat16), got_rows, preferred_element_type=jnp.float32
    ).astype(jnp.bfloat16).reshape(group_count * CROSS_CAP, square)
    mine_target = jnp.sum(jnp.where(picks, got_target[:, None, :], 0), axis=2)
    mine_slot = jnp.where(
        jnp.any(picks, axis=2), my_dom * slots_dev + mine_target, -1
    ).reshape(-1)

    inner_y = one_sided(face_in, restrictor(pick_rows(source_in, metric), orient_in))
    peer_i = peer_in[:, 0]
    inner_row_side = plain_restrictor(
        pick_rows(peer_i * elem_count + target_in // 3, metric_dom)
    )
    inner_c = coarse_terms(inner_row_side, inner_y).reshape(inner_count, square)
    inner_slot = peer_i * slots_dev + target_in

    slots = jnp.concatenate((inner_slot, mine_slot), axis=0)
    valid = slots >= 0
    slot_code = jnp.stack(
        (jnp.where(valid, slots // 32, -1), jnp.where(valid, slots % 32, 0)), axis=1
    )
    face_packet = jnp.concatenate(
        (inner_c.astype(jnp.bfloat16), mine_rows, id_row(slot_code, square)), axis=0
    )
    face_all = lax.all_gather(face_packet, "dom", axis=0)
    contrib_count = slots.shape[0]
    contrib = face_all[:, :contrib_count, :].reshape(group_width * contrib_count, square)
    codes = face_all[:, contrib_count, : 2 * contrib_count].astype(jnp.int32)
    hi = codes[:, 0::2].reshape(-1)
    lo = codes[:, 1::2].reshape(-1)
    got_slot = jnp.where(hi >= 0, hi * 32 + lo, -1)
    group_slots = group_width * slots_dev
    group_elems = group_width * elem_count
    faces = []
    for slot in range(3):
        onehot = (
            (jnp.arange(group_elems, dtype=jnp.int32) * 3 + slot)[:, None] == got_slot[None, :]
        ).astype(jnp.bfloat16)
        faces.append(jnp.dot(onehot, contrib, preferred_element_type=jnp.float32))
    face = jnp.concatenate(faces, axis=1)

    coarse_diag = diag_all.astype(jnp.float32)
    coarse_face = face.reshape(group_width * elem_count, 3 * square)
    return (coarse_diag, coarse_face)


def solution(mesh):
    placed = (
        P(("grp", "dom"), None, None),
        P(("grp", "dom"), None, None),
        P(("grp", "dom"), None, None),
        P(("grp", "dom"), None),
        P(("grp", "dom")),
        P(("grp", "dom")),
        P(("grp", "dom")),
        P(("grp", "dom")),
        P(("grp", "dom"), None),
        P(("grp", "dom"), None),
        P(("grp", "dom")),
        P(("grp", "dom")),
    )
    return jax.shard_map(
        per_device,
        mesh=mesh,
        in_specs=placed,
        out_specs=(P("grp", None), P("grp", None)),
        check_vma=False,
    )
```

```python
import jax
import jax.numpy as jnp
from jax import lax
from jax.sharding import PartitionSpec as P
from jax.experimental import pallas as pl
from jax.experimental.pallas import tpu as pltpu

CROSS_CAP = 3


def corner_table(var_count):
    nodes = -1.0 + 2.0 * jnp.arange(4, dtype=jnp.float32) / 3.0
    basis = jnp.stack(((1.0 - nodes) / 2.0, (1.0 + nodes) / 2.0), axis=1)
    cube = jnp.einsum("ia,jb,kc->abcijk", basis, basis, basis).reshape(8, 64)
    return jnp.kron(jnp.eye(var_count, dtype=jnp.float32), cube)


def restrictor(weights, orient):
    var_count = weights.shape[1] // 64
    table = corner_table(var_count)
    full = weights[:, None, :] * table[None]
    shaped = full.reshape(weights.shape[0], var_count * 8, var_count, 4, 4, 4)
    bits = orient.reshape(-1, 1, 1, 1, 1, 1)
    shaped = jnp.where(bits % 2 == 1, jnp.flip(shaped, 3), shaped)
    shaped = jnp.where(bits // 2 % 2 == 1, jnp.flip(shaped, 4), shaped)
    shaped = jnp.where(bits // 4 % 2 == 1, jnp.flip(shaped, 5), shaped)
    return shaped.reshape(weights.shape[0], var_count * 8, var_count * 64).astype(jnp.bfloat16)


def plain_restrictor(weights):
    table = corner_table(weights.shape[1] // 64)
    return (weights[:, None, :] * table[None]).astype(jnp.bfloat16)


def pick_rows(index, table):
    picks = (index[:, None] == jnp.arange(table.shape[0], dtype=jnp.int32)[None, :]).astype(
        jnp.float32
    )
    return jnp.dot(picks, table, precision=lax.Precision.HIGHEST)


def one_sided(blocks, column_side):
    return jnp.einsum(
        "rcj,rij->rci", column_side, blocks, preferred_element_type=jnp.float32
    ).astype(jnp.bfloat16)


def coarse_terms(row_side, products):
    return jnp.einsum("rci,rdi->rcd", row_side, products, preferred_element_type=jnp.float32)


def direct_gather(x, axes, order, collective_id):
    sizes = [lax.axis_size(axis) for axis in axes]

    def device(axis, peer):
        return tuple(peer if name == axis else lax.axis_index(name) for name in order)

    def kernel(x_ref, *rest):
        outs = rest[: len(axes)]
        send_sem, recv_sem, local_sem = rest[len(axes):]
        barrier = pltpu.get_barrier_semaphore()
        for axis, n in zip(axes, sizes):
            me = lax.axis_index(axis)
            for step in range(1, n):
                pl.semaphore_signal(
                    barrier, 1, device_id=device(axis, lax.rem(me + step, n)),
                    device_id_type=pl.DeviceIdType.MESH,
                )
        pl.semaphore_wait(barrier, sum(n - 1 for n in sizes))
        locals_ = []
        sends = []
        base = 0
        for a, (axis, n) in enumerate(zip(axes, sizes)):
            me = lax.axis_index(axis)
            local = pltpu.make_async_copy(x_ref, outs[a].at[me], local_sem.at[a])
            local.start()
            locals_.append(local)
            for step in range(1, n):
                copy = pltpu.make_async_remote_copy(
                    src_ref=x_ref,
                    dst_ref=outs[a].at[me],
                    send_sem=send_sem.at[base + step],
                    recv_sem=recv_sem.at[base + step],
                    device_id=device(axis, lax.rem(me + step, n)),
                    device_id_type=pl.DeviceIdType.MESH,
                )
                copy.start()
                sends.append(copy)
            base += n
        for copy in sends:
            copy.wait_send()
        base = 0
        for a, (axis, n) in enumerate(zip(axes, sizes)):
            me = lax.axis_index(axis)
            for step in range(1, n):
                source = lax.rem(me - step + n, n)
                pltpu.make_async_remote_copy(
                    src_ref=x_ref,
                    dst_ref=outs[a].at[source],
                    send_sem=send_sem.at[base + step],
                    recv_sem=recv_sem.at[base + step],
                    device_id=device(axis, source),
                    device_id_type=pl.DeviceIdType.MESH,
                ).wait_recv()
            base += n
        for local in locals_:
            local.wait()

    total = sum(sizes)
    return pl.pallas_call(
        kernel,
        out_shape=tuple(jax.ShapeDtypeStruct((n,) + x.shape, x.dtype) for n in sizes),
        in_specs=[pl.BlockSpec(memory_space=pl.ANY)],
        out_specs=tuple(pl.BlockSpec(memory_space=pl.ANY) for _ in sizes),
        scratch_shapes=[
            pltpu.SemaphoreType.DMA((total,)),
            pltpu.SemaphoreType.DMA((total,)),
            pltpu.SemaphoreType.DMA((len(axes),)),
        ],
        compiler_params=pltpu.CompilerParams(
            collective_id=collective_id, has_side_effects=True
        ),
    )(x)


def id_row(values, width):
    flat = values.reshape(-1).astype(jnp.bfloat16)
    return jnp.pad(flat, (0, width - flat.shape[0]))[None, :]


def per_device(
    diag_blocks,
    face_in,
    face_cross,
    metric,
    source_in,
    source_cross,
    orient_in,
    orient_cross,
    peer_in,
    peer_cross,
    target_in,
    target_cross,
):
    elem_count = metric.shape[0]
    coarse_width = metric.shape[1] // 8
    square = coarse_width * coarse_width
    slots_dev = 3 * elem_count
    group_width = lax.axis_size("dom")
    group_count = lax.axis_size("grp")
    my_dom = lax.axis_index("dom")
    my_grp = lax.axis_index("grp")
    inner_count = face_in.shape[0]
    cross_count = face_cross.shape[0]

    order = ("grp", "dom")
    metric_dom, metric_grp = direct_gather(metric, ("dom", "grp"), order, 0)
    metric_dom = metric_dom.reshape(-1, metric.shape[1])
    metric_grp = metric_grp.reshape(-1, metric.shape[1])

    diag_side = plain_restrictor(metric)
    diag_c = coarse_terms(diag_side, one_sided(diag_blocks, diag_side))
    diag_rows = diag_c.reshape(elem_count, square).astype(jnp.bfloat16)

    cross_y = one_sided(face_cross, restrictor(pick_rows(source_cross, metric), orient_cross))
    peer_x = peer_cross[:, 0]
    cross_row_side = plain_restrictor(
        pick_rows(peer_x * elem_count + target_cross // 3, metric_grp)
    )
    cross_c = coarse_terms(cross_row_side, cross_y).reshape(cross_count, square)
    cross_ids = jnp.stack((peer_x, target_cross), axis=1)
    cross_packet = jnp.concatenate(
        (cross_c.astype(jnp.bfloat16), id_row(cross_ids, square)), axis=0
    )
    (cross_got,) = direct_gather(cross_packet, ("grp",), order, 1)
    got_rows = cross_got[:, :cross_count, :]
    got_ids = cross_got[:, cross_count, : 2 * cross_count].astype(jnp.int32)
    got_peer = got_ids[:, 0::2]
    got_target = got_ids[:, 1::2]
    match = got_peer == my_grp
    rank = jnp.cumsum(match.astype(jnp.int32), axis=1) - 1
    picks = match[:, None, :] & (
        rank[:, None, :] == jnp.arange(CROSS_CAP, dtype=jnp.int32)[None, :, None]
    )
    mine_rows = jnp.einsum(
        "skr,srq->skq", picks.astype(jnp.bfloat16), got_rows, preferred_element_type=jnp.float32
    ).astype(jnp.bfloat16).reshape(group_count * CROSS_CAP, square)
    mine_target = jnp.sum(jnp.where(picks, got_target[:, None, :], 0), axis=2)
    mine_slot = jnp.where(
        jnp.any(picks, axis=2), my_dom * slots_dev + mine_target, -1
    ).reshape(-1)

    inner_y = one_sided(face_in, restrictor(pick_rows(source_in, metric), orient_in))
    peer_i = peer_in[:, 0]
    inner_row_side = plain_restrictor(
        pick_rows(peer_i * elem_count + target_in // 3, metric_dom)
    )
    inner_c = coarse_terms(inner_row_side, inner_y).reshape(inner_count, square)
    inner_slot = peer_i * slots_dev + target_in

    slots = jnp.concatenate((inner_slot, mine_slot), axis=0)
    valid = slots >= 0
    slot_code = jnp.stack(
        (jnp.where(valid, slots // 32, -1), jnp.where(valid, slots % 32, 0)), axis=1
    )
    face_packet = jnp.concatenate(
        (id_row(slot_code, square), diag_rows, inner_c.astype(jnp.bfloat16), mine_rows), axis=0
    )
    face_all = lax.all_gather(face_packet, "dom", axis=0)
    contrib_count = slots.shape[0]
    packet_rows = face_packet.shape[0]
    contrib = face_all.reshape(group_width * packet_rows, square)
    codes = face_all[:, 0, : 2 * contrib_count].astype(jnp.int32)
    hi = jnp.pad(codes[:, 0::2], ((0, 0), (1 + elem_count, 0)), constant_values=-1).reshape(-1)
    lo = jnp.pad(codes[:, 1::2], ((0, 0), (1 + elem_count, 0))).reshape(-1)
    got_slot = jnp.where(hi >= 0, hi * 32 + lo, -1)
    group_slots = group_width * slots_dev
    group_elems = group_width * elem_count
    faces = []
    for slot in range(3):
        onehot = (
            (jnp.arange(group_elems, dtype=jnp.int32) * 3 + slot)[:, None] == got_slot[None, :]
        ).astype(jnp.bfloat16)
        faces.append(jnp.dot(onehot, contrib, preferred_element_type=jnp.float32))
    face = jnp.concatenate(faces, axis=1)

    coarse_diag = face_all[:, 1 : 1 + elem_count, :].reshape(-1, square).astype(jnp.float32)
    coarse_face = face.reshape(group_width * elem_count, 3 * square)
    return (coarse_diag, coarse_face)


def solution(mesh):
    placed = (
        P(("grp", "dom"), None, None),
        P(("grp", "dom"), None, None),
        P(("grp", "dom"), None, None),
        P(("grp", "dom"), None),
        P(("grp", "dom")),
        P(("grp", "dom")),
        P(("grp", "dom")),
        P(("grp", "dom")),
        P(("grp", "dom"), None),
        P(("grp", "dom"), None),
        P(("grp", "dom")),
        P(("grp", "dom")),
    )
    return jax.shard_map(
        per_device,
        mesh=mesh,
        in_specs=placed,
        out_specs=(P("grp", None), P("grp", None)),
        check_vma=False,
    )
```

```python
import jax
import jax.numpy as jnp
from jax import lax
from jax.sharding import PartitionSpec as P
from jax.experimental import pallas as pl
from jax.experimental.pallas import tpu as pltpu

CROSS_CAP = 3


def corner_table(var_count):
    nodes = -1.0 + 2.0 * jnp.arange(4, dtype=jnp.float32) / 3.0
    basis = jnp.stack(((1.0 - nodes) / 2.0, (1.0 + nodes) / 2.0), axis=1)
    cube = jnp.einsum("ia,jb,kc->abcijk", basis, basis, basis).reshape(8, 64)
    return jnp.kron(jnp.eye(var_count, dtype=jnp.float32), cube)


def restrictor(weights, orient):
    var_count = weights.shape[1] // 64
    table = corner_table(var_count)
    full = weights[:, None, :] * table[None]
    shaped = full.reshape(weights.shape[0], var_count * 8, var_count, 4, 4, 4)
    bits = orient.reshape(-1, 1, 1, 1, 1, 1)
    shaped = jnp.where(bits % 2 == 1, jnp.flip(shaped, 3), shaped)
    shaped = jnp.where(bits // 2 % 2 == 1, jnp.flip(shaped, 4), shaped)
    shaped = jnp.where(bits // 4 % 2 == 1, jnp.flip(shaped, 5), shaped)
    return shaped.reshape(weights.shape[0], var_count * 8, var_count * 64).astype(jnp.bfloat16)


def plain_restrictor(weights):
    table = corner_table(weights.shape[1] // 64)
    return (weights[:, None, :] * table[None]).astype(jnp.bfloat16)


def pick_rows(index, table):
    picks = (index[:, None] == jnp.arange(table.shape[0], dtype=jnp.int32)[None, :]).astype(
        jnp.float32
    )
    return jnp.dot(picks, table, precision=lax.Precision.HIGHEST)


def one_sided(blocks, column_side):
    return jnp.einsum(
        "rcj,rij->rci", column_side, blocks, preferred_element_type=jnp.float32
    ).astype(jnp.bfloat16)


def coarse_terms(row_side, products):
    return jnp.einsum("rci,rdi->rcd", row_side, products, preferred_element_type=jnp.float32)


def direct_gather(x, axes, order, collective_id):
    sizes = [lax.axis_size(axis) for axis in axes]

    def device(axis, peer):
        return tuple(peer if name == axis else lax.axis_index(name) for name in order)

    def kernel(x_ref, *rest):
        outs = rest[: len(axes)]
        send_sem, recv_sem, local_sem = rest[len(axes):]
        barrier = pltpu.get_barrier_semaphore()
        for axis, n in zip(axes, sizes):
            me = lax.axis_index(axis)
            for step in range(1, n):
                pl.semaphore_signal(
                    barrier, 1, device_id=device(axis, lax.rem(me + step, n)),
                    device_id_type=pl.DeviceIdType.MESH,
                )
        pl.semaphore_wait(barrier, sum(n - 1 for n in sizes))
        locals_ = []
        sends = []
        base = 0
        for a, (axis, n) in enumerate(zip(axes, sizes)):
            me = lax.axis_index(axis)
            local = pltpu.make_async_copy(x_ref, outs[a].at[me], local_sem.at[a])
            local.start()
            locals_.append(local)
            for step in range(1, n):
                copy = pltpu.make_async_remote_copy(
                    src_ref=x_ref,
                    dst_ref=outs[a].at[me],
                    send_sem=send_sem.at[base + step],
                    recv_sem=recv_sem.at[base + step],
                    device_id=device(axis, lax.rem(me + step, n)),
                    device_id_type=pl.DeviceIdType.MESH,
                )
                copy.start()
                sends.append(copy)
            base += n
        for copy in sends:
            copy.wait_send()
        base = 0
        for a, (axis, n) in enumerate(zip(axes, sizes)):
            me = lax.axis_index(axis)
            for step in range(1, n):
                source = lax.rem(me - step + n, n)
                pltpu.make_async_remote_copy(
                    src_ref=x_ref,
                    dst_ref=outs[a].at[source],
                    send_sem=send_sem.at[base + step],
                    recv_sem=recv_sem.at[base + step],
                    device_id=device(axis, source),
                    device_id_type=pl.DeviceIdType.MESH,
                ).wait_recv()
            base += n
        for local in locals_:
            local.wait()

    total = sum(sizes)
    return pl.pallas_call(
        kernel,
        out_shape=tuple(jax.ShapeDtypeStruct((n,) + x.shape, x.dtype) for n in sizes),
        in_specs=[pl.BlockSpec(memory_space=pl.ANY)],
        out_specs=tuple(pl.BlockSpec(memory_space=pl.ANY) for _ in sizes),
        scratch_shapes=[
            pltpu.SemaphoreType.DMA((total,)),
            pltpu.SemaphoreType.DMA((total,)),
            pltpu.SemaphoreType.DMA((len(axes),)),
        ],
        compiler_params=pltpu.CompilerParams(
            collective_id=collective_id, has_side_effects=True
        ),
    )(x)


def id_row(values, width):
    flat = values.reshape(-1).astype(jnp.bfloat16)
    return jnp.pad(flat, (0, width - flat.shape[0]))[None, :]


def per_device(
    diag_blocks,
    face_in,
    face_cross,
    metric,
    source_in,
    source_cross,
    orient_in,
    orient_cross,
    peer_in,
    peer_cross,
    target_in,
    target_cross,
):
    elem_count = metric.shape[0]
    coarse_width = metric.shape[1] // 8
    square = coarse_width * coarse_width
    slots_dev = 3 * elem_count
    group_width = lax.axis_size("dom")
    group_count = lax.axis_size("grp")
    my_dom = lax.axis_index("dom")
    my_grp = lax.axis_index("grp")
    inner_count = face_in.shape[0]
    cross_count = face_cross.shape[0]

    order = ("grp", "dom")
    peer_x = peer_cross[:, 0]
    peer_i = peer_in[:, 0]
    id_cols = jnp.zeros((elem_count, 128), jnp.float32)
    id_cols = id_cols.at[:cross_count, 0].set(peer_x.astype(jnp.float32))
    id_cols = id_cols.at[:cross_count, 1].set(target_cross.astype(jnp.float32))
    metric_ids = jnp.concatenate((metric, id_cols), axis=1)
    fine = metric.shape[1]
    dom_got, grp_got = direct_gather(metric_ids, ("dom", "grp"), order, 0)
    metric_dom = dom_got[:, :, :fine].reshape(-1, fine)
    metric_grp = grp_got[:, :, :fine].reshape(-1, fine)
    got_peer = grp_got[:, :cross_count, fine].astype(jnp.int32)
    got_target = grp_got[:, :cross_count, fine + 1].astype(jnp.int32)

    match = got_peer == my_grp
    rank = jnp.cumsum(match.astype(jnp.int32), axis=1) - 1
    picks = match[:, None, :] & (
        rank[:, None, :] == jnp.arange(CROSS_CAP, dtype=jnp.int32)[None, :, None]
    )
    mine_target = jnp.sum(jnp.where(picks, got_target[:, None, :], 0), axis=2)
    mine_slot = jnp.where(
        jnp.any(picks, axis=2), my_dom * slots_dev + mine_target, -1
    ).reshape(-1)
    inner_slot = peer_i * slots_dev + target_in
    slots = jnp.concatenate((inner_slot, mine_slot), axis=0)
    valid = slots >= 0
    slot_code = jnp.stack(
        (jnp.where(valid, slots // 32, -1), jnp.where(valid, slots % 32, 0)), axis=1
    )

    diag_side = plain_restrictor(metric)
    diag_c = coarse_terms(diag_side, one_sided(diag_blocks, diag_side))
    diag_rows = diag_c.reshape(elem_count, square).astype(jnp.bfloat16)
    diag_packet = jnp.concatenate((diag_rows, id_row(slot_code, square)), axis=0)
    diag_all = lax.all_gather(diag_packet, "dom", axis=0)

    cross_y = one_sided(face_cross, restrictor(pick_rows(source_cross, metric), orient_cross))
    cross_row_side = plain_restrictor(
        pick_rows(peer_x * elem_count + target_cross // 3, metric_grp)
    )
    cross_c = coarse_terms(cross_row_side, cross_y).reshape(cross_count, square)
    (got_rows,) = direct_gather(cross_c.astype(jnp.bfloat16), ("grp",), order, 1)
    mine_rows = jnp.einsum(
        "skr,srq->skq", picks.astype(jnp.bfloat16), got_rows, preferred_element_type=jnp.float32
    ).astype(jnp.bfloat16).reshape(group_count * CROSS_CAP, square)

    inner_y = one_sided(face_in, restrictor(pick_rows(source_in, metric), orient_in))
    inner_row_side = plain_restrictor(
        pick_rows(peer_i * elem_count + target_in // 3, metric_dom)
    )
    inner_c = coarse_terms(inner_row_side, inner_y).reshape(inner_count, square)

    face_packet = jnp.concatenate((inner_c.astype(jnp.bfloat16), mine_rows), axis=0)
    face_all = lax.all_gather(face_packet, "dom", axis=0)
    contrib_count = slots.shape[0]
    codes = diag_all[:, elem_count, : 2 * contrib_count].astype(jnp.int32)
    hi = codes[:, 0::2]
    lo = codes[:, 1::2]
    got_slot = jnp.where(hi >= 0, hi * 32 + lo, -1)
    group_elems = group_width * elem_count
    faces = []
    for slot in range(3):
        onehot = (
            (jnp.arange(group_elems, dtype=jnp.int32) * 3 + slot)[:, None, None]
            == got_slot[None, :, :]
        ).astype(jnp.bfloat16)
        faces.append(
            jnp.einsum("sdr,drq->sq", onehot, face_all, preferred_element_type=jnp.float32)
        )
    face = jnp.concatenate(faces, axis=1)

    coarse_diag = diag_all[:, :elem_count, :].reshape(-1, square).astype(jnp.float32)
    coarse_face = face.reshape(group_width * elem_count, 3 * square)
    return (coarse_diag, coarse_face)


def solution(mesh):
    placed = (
        P(("grp", "dom"), None, None),
        P(("grp", "dom"), None, None),
        P(("grp", "dom"), None, None),
        P(("grp", "dom"), None),
        P(("grp", "dom")),
        P(("grp", "dom")),
        P(("grp", "dom")),
        P(("grp", "dom")),
        P(("grp", "dom"), None),
        P(("grp", "dom"), None),
        P(("grp", "dom")),
        P(("grp", "dom")),
    )
    return jax.shard_map(
        per_device,
        mesh=mesh,
        in_specs=placed,
        out_specs=(P("grp", None), P("grp", None)),
        check_vma=False,
    )
```

```python
import jax
import jax.numpy as jnp
from jax import lax
from jax.sharding import PartitionSpec as P
from jax.experimental import pallas as pl
from jax.experimental.pallas import tpu as pltpu

CROSS_CAP = 3


def corner_table(var_count):
    nodes = -1.0 + 2.0 * jnp.arange(4, dtype=jnp.float32) / 3.0
    basis = jnp.stack(((1.0 - nodes) / 2.0, (1.0 + nodes) / 2.0), axis=1)
    cube = jnp.einsum("ia,jb,kc->abcijk", basis, basis, basis).reshape(8, 64)
    return jnp.kron(jnp.eye(var_count, dtype=jnp.float32), cube)


def restrictor(weights, orient):
    var_count = weights.shape[1] // 64
    table = corner_table(var_count)
    full = weights[:, None, :] * table[None]
    shaped = full.reshape(weights.shape[0], var_count * 8, var_count, 4, 4, 4)
    bits = orient.reshape(-1, 1, 1, 1, 1, 1)
    shaped = jnp.where(bits % 2 == 1, jnp.flip(shaped, 3), shaped)
    shaped = jnp.where(bits // 2 % 2 == 1, jnp.flip(shaped, 4), shaped)
    shaped = jnp.where(bits // 4 % 2 == 1, jnp.flip(shaped, 5), shaped)
    return shaped.reshape(weights.shape[0], var_count * 8, var_count * 64).astype(jnp.bfloat16)


def plain_restrictor(weights):
    table = corner_table(weights.shape[1] // 64)
    return (weights[:, None, :] * table[None]).astype(jnp.bfloat16)


def pick_rows(index, table):
    picks = (index[:, None] == jnp.arange(table.shape[0], dtype=jnp.int32)[None, :]).astype(
        jnp.float32
    )
    return jnp.dot(picks, table, precision=lax.Precision.HIGHEST)


def one_sided(blocks, column_side):
    return jnp.einsum(
        "rcj,rij->rci", column_side, blocks, preferred_element_type=jnp.float32
    ).astype(jnp.bfloat16)


def coarse_terms(row_side, products):
    return jnp.einsum("rci,rdi->rcd", row_side, products, preferred_element_type=jnp.float32)


def direct_gather(x, axes, order, collective_id):
    sizes = [lax.axis_size(axis) for axis in axes]

    def device(axis, peer):
        return tuple(peer if name == axis else lax.axis_index(name) for name in order)

    def kernel(x_ref, *rest):
        outs = rest[: len(axes)]
        send_sem, recv_sem, local_sem = rest[len(axes):]
        barrier = pltpu.get_barrier_semaphore()
        for axis, n in zip(axes, sizes):
            me = lax.axis_index(axis)
            for step in range(1, n):
                pl.semaphore_signal(
                    barrier, 1, device_id=device(axis, lax.rem(me + step, n)),
                    device_id_type=pl.DeviceIdType.MESH,
                )
        pl.semaphore_wait(barrier, sum(n - 1 for n in sizes))
        locals_ = []
        sends = []
        base = 0
        for a, (axis, n) in enumerate(zip(axes, sizes)):
            me = lax.axis_index(axis)
            local = pltpu.make_async_copy(x_ref, outs[a].at[me], local_sem.at[a])
            local.start()
            locals_.append(local)
            for step in range(1, n):
                copy = pltpu.make_async_remote_copy(
                    src_ref=x_ref,
                    dst_ref=outs[a].at[me],
                    send_sem=send_sem.at[base + step],
                    recv_sem=recv_sem.at[base + step],
                    device_id=device(axis, lax.rem(me + step, n)),
                    device_id_type=pl.DeviceIdType.MESH,
                )
                copy.start()
                sends.append(copy)
            base += n
        for copy in sends:
            copy.wait_send()
        base = 0
        for a, (axis, n) in enumerate(zip(axes, sizes)):
            me = lax.axis_index(axis)
            for step in range(1, n):
                source = lax.rem(me - step + n, n)
                pltpu.make_async_remote_copy(
                    src_ref=x_ref,
                    dst_ref=outs[a].at[source],
                    send_sem=send_sem.at[base + step],
                    recv_sem=recv_sem.at[base + step],
                    device_id=device(axis, source),
                    device_id_type=pl.DeviceIdType.MESH,
                ).wait_recv()
            base += n
        for local in locals_:
            local.wait()

    total = sum(sizes)
    return pl.pallas_call(
        kernel,
        out_shape=tuple(jax.ShapeDtypeStruct((n,) + x.shape, x.dtype) for n in sizes),
        in_specs=[pl.BlockSpec(memory_space=pl.ANY)],
        out_specs=tuple(pl.BlockSpec(memory_space=pl.ANY) for _ in sizes),
        scratch_shapes=[
            pltpu.SemaphoreType.DMA((total,)),
            pltpu.SemaphoreType.DMA((total,)),
            pltpu.SemaphoreType.DMA((len(axes),)),
        ],
        compiler_params=pltpu.CompilerParams(
            collective_id=collective_id, has_side_effects=True
        ),
    )(x)


def id_row(values, width):
    flat = values.reshape(-1).astype(jnp.bfloat16)
    return jnp.pad(flat, (0, width - flat.shape[0]))[None, :]


def per_device(
    diag_blocks,
    face_in,
    face_cross,
    metric,
    source_in,
    source_cross,
    orient_in,
    orient_cross,
    peer_in,
    peer_cross,
    target_in,
    target_cross,
):
    elem_count = metric.shape[0]
    coarse_width = metric.shape[1] // 8
    square = coarse_width * coarse_width
    slots_dev = 3 * elem_count
    group_width = lax.axis_size("dom")
    group_count = lax.axis_size("grp")
    my_dom = lax.axis_index("dom")
    my_grp = lax.axis_index("grp")
    inner_count = face_in.shape[0]
    cross_count = face_cross.shape[0]

    order = ("grp", "dom")
    peer_x = peer_cross[:, 0]
    peer_i = peer_in[:, 0]
    id_cols = jnp.zeros((elem_count, 128), jnp.float32)
    id_cols = id_cols.at[:cross_count, 0].set(peer_x.astype(jnp.float32))
    id_cols = id_cols.at[:cross_count, 1].set(target_cross.astype(jnp.float32))
    metric_ids = jnp.concatenate((metric, id_cols), axis=1)
    fine = metric.shape[1]
    dom_got, grp_got = direct_gather(metric_ids, ("dom", "grp"), order, 0)
    metric_dom = dom_got[:, :, :fine].reshape(-1, fine)
    metric_grp = grp_got[:, :, :fine].reshape(-1, fine)
    got_peer = grp_got[:, :cross_count, fine].astype(jnp.int32)
    got_target = grp_got[:, :cross_count, fine + 1].astype(jnp.int32)

    match = got_peer == my_grp
    rank = jnp.cumsum(match.astype(jnp.int32), axis=1) - 1
    picks = match[:, None, :] & (
        rank[:, None, :] == jnp.arange(CROSS_CAP, dtype=jnp.int32)[None, :, None]
    )
    mine_target = jnp.sum(jnp.where(picks, got_target[:, None, :], 0), axis=2)
    mine_slot = jnp.where(
        jnp.any(picks, axis=2), my_dom * slots_dev + mine_target, -1
    ).reshape(-1)
    inner_slot = peer_i * slots_dev + target_in
    slots = jnp.concatenate((inner_slot, mine_slot), axis=0)
    valid = slots >= 0
    slot_code = jnp.stack(
        (jnp.where(valid, slots // 32, -1), jnp.where(valid, slots % 32, 0)), axis=1
    )

    diag_side = plain_restrictor(metric)
    diag_c = coarse_terms(diag_side, one_sided(diag_blocks, diag_side))
    diag_rows = diag_c.reshape(elem_count, square).astype(jnp.bfloat16)
    diag_all = lax.all_gather(diag_rows, "dom", axis=0)

    cross_y = one_sided(face_cross, restrictor(pick_rows(source_cross, metric), orient_cross))
    cross_row_side = plain_restrictor(
        pick_rows(peer_x * elem_count + target_cross // 3, metric_grp)
    )
    cross_c = coarse_terms(cross_row_side, cross_y).reshape(cross_count, square)
    (got_rows,) = direct_gather(cross_c.astype(jnp.bfloat16), ("grp",), order, 1)
    mine_rows = jnp.einsum(
        "skr,srq->skq", picks.astype(jnp.bfloat16), got_rows, preferred_element_type=jnp.float32
    ).astype(jnp.bfloat16).reshape(group_count * CROSS_CAP, square)

    inner_y = one_sided(face_in, restrictor(pick_rows(source_in, metric), orient_in))
    inner_row_side = plain_restrictor(
        pick_rows(peer_i * elem_count + target_in // 3, metric_dom)
    )
    inner_c = coarse_terms(inner_row_side, inner_y).reshape(inner_count, square)

    face_packet = jnp.concatenate(
        (inner_c.astype(jnp.bfloat16), id_row(slot_code, square)), axis=0
    )
    face_all = lax.all_gather(face_packet, "dom", axis=0)
    (cross_all,) = direct_gather(mine_rows, ("dom",), order, 2)
    contrib_count = slots.shape[0]
    codes = face_all[:, inner_count, : 2 * contrib_count].astype(jnp.int32)
    got_slot = jnp.where(codes[:, 0::2] >= 0, codes[:, 0::2] * 32 + codes[:, 1::2], -1)
    inner_got = jnp.pad(got_slot[:, :inner_count], ((0, 0), (0, 1)), constant_values=-1)
    cross_got = got_slot[:, inner_count:]
    group_elems = group_width * elem_count
    faces = []
    for slot in range(3):
        wanted = (jnp.arange(group_elems, dtype=jnp.int32) * 3 + slot)[:, None, None]
        from_inner = jnp.einsum(
            "sdr,drq->sq", (wanted == inner_got[None]).astype(jnp.bfloat16), face_all,
            preferred_element_type=jnp.float32,
        )
        from_cross = jnp.einsum(
            "sdr,drq->sq", (wanted == cross_got[None]).astype(jnp.bfloat16), cross_all,
            preferred_element_type=jnp.float32,
        )
        faces.append(from_inner + from_cross)
    face = jnp.concatenate(faces, axis=1)

    coarse_diag = diag_all[:, :elem_count, :].reshape(-1, square).astype(jnp.float32)
    coarse_face = face.reshape(group_width * elem_count, 3 * square)
    return (coarse_diag, coarse_face)


def solution(mesh):
    placed = (
        P(("grp", "dom"), None, None),
        P(("grp", "dom"), None, None),
        P(("grp", "dom"), None, None),
        P(("grp", "dom"), None),
        P(("grp", "dom")),
        P(("grp", "dom")),
        P(("grp", "dom")),
        P(("grp", "dom")),
        P(("grp", "dom"), None),
        P(("grp", "dom"), None),
        P(("grp", "dom")),
        P(("grp", "dom")),
    )
    return jax.shard_map(
        per_device,
        mesh=mesh,
        in_specs=placed,
        out_specs=(P("grp", None), P("grp", None)),
        check_vma=False,
    )
```

```python
import jax
import jax.numpy as jnp
from jax import lax
from jax.sharding import PartitionSpec as P
from jax.experimental import pallas as pl
from jax.experimental.pallas import tpu as pltpu

CROSS_CAP = 3


def corner_table(var_count):
    nodes = -1.0 + 2.0 * jnp.arange(4, dtype=jnp.float32) / 3.0
    basis = jnp.stack(((1.0 - nodes) / 2.0, (1.0 + nodes) / 2.0), axis=1)
    cube = jnp.einsum("ia,jb,kc->abcijk", basis, basis, basis).reshape(8, 64)
    return jnp.kron(jnp.eye(var_count, dtype=jnp.float32), cube)


def restrictor(weights, orient):
    var_count = weights.shape[1] // 64
    table = corner_table(var_count)
    full = weights[:, None, :] * table[None]
    shaped = full.reshape(weights.shape[0], var_count * 8, var_count, 4, 4, 4)
    bits = orient.reshape(-1, 1, 1, 1, 1, 1)
    shaped = jnp.where(bits % 2 == 1, jnp.flip(shaped, 3), shaped)
    shaped = jnp.where(bits // 2 % 2 == 1, jnp.flip(shaped, 4), shaped)
    shaped = jnp.where(bits // 4 % 2 == 1, jnp.flip(shaped, 5), shaped)
    return shaped.reshape(weights.shape[0], var_count * 8, var_count * 64).astype(jnp.bfloat16)


def plain_restrictor(weights):
    table = corner_table(weights.shape[1] // 64)
    return (weights[:, None, :] * table[None]).astype(jnp.bfloat16)


def pick_rows(index, table):
    picks = (index[:, None] == jnp.arange(table.shape[0], dtype=jnp.int32)[None, :]).astype(
        jnp.float32
    )
    return jnp.dot(picks, table, precision=lax.Precision.HIGHEST)


def one_sided(blocks, column_side):
    return jnp.einsum(
        "rcj,rij->rci", column_side, blocks, preferred_element_type=jnp.float32
    ).astype(jnp.bfloat16)


def coarse_terms(row_side, products):
    return jnp.einsum("rci,rdi->rcd", row_side, products, preferred_element_type=jnp.float32)


def direct_gather(x, axes, order, collective_id):
    sizes = [lax.axis_size(axis) for axis in axes]

    def device(axis, peer):
        return tuple(peer if name == axis else lax.axis_index(name) for name in order)

    def kernel(x_ref, *rest):
        outs = rest[: len(axes)]
        send_sem, recv_sem, local_sem = rest[len(axes):]
        barrier = pltpu.get_barrier_semaphore()
        for axis, n in zip(axes, sizes):
            me = lax.axis_index(axis)
            for step in range(1, n):
                pl.semaphore_signal(
                    barrier, 1, device_id=device(axis, lax.rem(me + step, n)),
                    device_id_type=pl.DeviceIdType.MESH,
                )
        pl.semaphore_wait(barrier, sum(n - 1 for n in sizes))
        locals_ = []
        sends = []
        base = 0
        for a, (axis, n) in enumerate(zip(axes, sizes)):
            me = lax.axis_index(axis)
            local = pltpu.make_async_copy(x_ref, outs[a].at[me], local_sem.at[a])
            local.start()
            locals_.append(local)
            for step in range(1, n):
                copy = pltpu.make_async_remote_copy(
                    src_ref=x_ref,
                    dst_ref=outs[a].at[me],
                    send_sem=send_sem.at[base + step],
                    recv_sem=recv_sem.at[base + step],
                    device_id=device(axis, lax.rem(me + step, n)),
                    device_id_type=pl.DeviceIdType.MESH,
                )
                copy.start()
                sends.append(copy)
            base += n
        for copy in sends:
            copy.wait_send()
        base = 0
        for a, (axis, n) in enumerate(zip(axes, sizes)):
            me = lax.axis_index(axis)
            for step in range(1, n):
                source = lax.rem(me - step + n, n)
                pltpu.make_async_remote_copy(
                    src_ref=x_ref,
                    dst_ref=outs[a].at[source],
                    send_sem=send_sem.at[base + step],
                    recv_sem=recv_sem.at[base + step],
                    device_id=device(axis, source),
                    device_id_type=pl.DeviceIdType.MESH,
                ).wait_recv()
            base += n
        for local in locals_:
            local.wait()

    total = sum(sizes)
    return pl.pallas_call(
        kernel,
        out_shape=tuple(jax.ShapeDtypeStruct((n,) + x.shape, x.dtype) for n in sizes),
        in_specs=[pl.BlockSpec(memory_space=pl.ANY)],
        out_specs=tuple(pl.BlockSpec(memory_space=pl.ANY) for _ in sizes),
        scratch_shapes=[
            pltpu.SemaphoreType.DMA((total,)),
            pltpu.SemaphoreType.DMA((total,)),
            pltpu.SemaphoreType.DMA((len(axes),)),
        ],
        compiler_params=pltpu.CompilerParams(
            collective_id=collective_id, has_side_effects=True
        ),
    )(x)


def slot_codes(slots):
    valid = slots >= 0
    return jnp.stack((jnp.where(valid, slots // 32, -1), jnp.where(valid, slots % 32, 0)), axis=1)


def read_codes(row, count):
    codes = row[:, : 2 * count].astype(jnp.int32)
    return jnp.where(codes[:, 0::2] >= 0, codes[:, 0::2] * 32 + codes[:, 1::2], -1)


def id_row(values, width):
    flat = values.reshape(-1).astype(jnp.bfloat16)
    return jnp.pad(flat, (0, width - flat.shape[0]))[None, :]


def per_device(
    diag_blocks,
    face_in,
    face_cross,
    metric,
    source_in,
    source_cross,
    orient_in,
    orient_cross,
    peer_in,
    peer_cross,
    target_in,
    target_cross,
):
    elem_count = metric.shape[0]
    coarse_width = metric.shape[1] // 8
    square = coarse_width * coarse_width
    slots_dev = 3 * elem_count
    group_width = lax.axis_size("dom")
    group_count = lax.axis_size("grp")
    my_dom = lax.axis_index("dom")
    my_grp = lax.axis_index("grp")
    inner_count = face_in.shape[0]
    cross_count = face_cross.shape[0]

    order = ("grp", "dom")
    peer_x = peer_cross[:, 0]
    peer_i = peer_in[:, 0]
    fine = metric.shape[1]
    (dom_got,) = direct_gather(metric, ("dom",), order, 0)
    metric_dom = dom_got.reshape(-1, fine)
    inner_slot = peer_i * slots_dev + target_in

    diag_side = plain_restrictor(metric)
    diag_c = coarse_terms(diag_side, one_sided(diag_blocks, diag_side))
    diag_rows = diag_c.reshape(elem_count, square).astype(jnp.bfloat16)
    diag_all = lax.all_gather(diag_rows, "dom", axis=0)

    id_cols = jnp.zeros((elem_count, 128), jnp.float32)
    id_cols = id_cols.at[:cross_count, 0].set(peer_x.astype(jnp.float32))
    id_cols = id_cols.at[:cross_count, 1].set(target_cross.astype(jnp.float32))
    (grp_got,) = direct_gather(jnp.concatenate((metric, id_cols), axis=1), ("grp",), order, 3)
    metric_grp = grp_got[:, :, :fine].reshape(-1, fine)
    got_peer = grp_got[:, :cross_count, fine].astype(jnp.int32)
    got_target = grp_got[:, :cross_count, fine + 1].astype(jnp.int32)
    match = got_peer == my_grp
    rank = jnp.cumsum(match.astype(jnp.int32), axis=1) - 1
    picks = match[:, None, :] & (
        rank[:, None, :] == jnp.arange(CROSS_CAP, dtype=jnp.int32)[None, :, None]
    )
    mine_target = jnp.sum(jnp.where(picks, got_target[:, None, :], 0), axis=2)
    mine_slot = jnp.where(
        jnp.any(picks, axis=2), my_dom * slots_dev + mine_target, -1
    ).reshape(-1)
    cross_y = one_sided(face_cross, restrictor(pick_rows(source_cross, metric), orient_cross))
    cross_row_side = plain_restrictor(
        pick_rows(peer_x * elem_count + target_cross // 3, metric_grp)
    )
    cross_c = coarse_terms(cross_row_side, cross_y).reshape(cross_count, square)
    (got_rows,) = direct_gather(cross_c.astype(jnp.bfloat16), ("grp",), order, 1)
    mine_rows = jnp.einsum(
        "skr,srq->skq", picks.astype(jnp.bfloat16), got_rows, preferred_element_type=jnp.float32
    ).astype(jnp.bfloat16).reshape(group_count * CROSS_CAP, square)

    inner_y = one_sided(face_in, restrictor(pick_rows(source_in, metric), orient_in))
    inner_row_side = plain_restrictor(
        pick_rows(peer_i * elem_count + target_in // 3, metric_dom)
    )
    inner_c = coarse_terms(inner_row_side, inner_y).reshape(inner_count, square)

    face_packet = jnp.concatenate(
        (inner_c.astype(jnp.bfloat16), id_row(slot_codes(inner_slot), square)), axis=0
    )
    face_all = lax.all_gather(face_packet, "dom", axis=0)
    cross_packet = jnp.concatenate((mine_rows, id_row(slot_codes(mine_slot), square)), axis=0)
    (cross_all,) = direct_gather(cross_packet, ("dom",), order, 2)
    inner_got = jnp.pad(
        read_codes(face_all[:, inner_count], inner_count), ((0, 0), (0, 1)), constant_values=-1
    )
    cross_got = jnp.pad(
        read_codes(cross_all[:, mine_rows.shape[0]], mine_rows.shape[0]),
        ((0, 0), (0, 1)), constant_values=-1,
    )
    group_elems = group_width * elem_count
    faces = []
    for slot in range(3):
        wanted = (jnp.arange(group_elems, dtype=jnp.int32) * 3 + slot)[:, None, None]
        from_inner = jnp.einsum(
            "sdr,drq->sq", (wanted == inner_got[None]).astype(jnp.bfloat16), face_all,
            preferred_element_type=jnp.float32,
        )
        from_cross = jnp.einsum(
            "sdr,drq->sq", (wanted == cross_got[None]).astype(jnp.bfloat16), cross_all,
            preferred_element_type=jnp.float32,
        )
        faces.append(from_inner + from_cross)
    face = jnp.concatenate(faces, axis=1)

    coarse_diag = diag_all[:, :elem_count, :].reshape(-1, square).astype(jnp.float32)
    coarse_face = face.reshape(group_width * elem_count, 3 * square)
    return (coarse_diag, coarse_face)


def solution(mesh):
    placed = (
        P(("grp", "dom"), None, None),
        P(("grp", "dom"), None, None),
        P(("grp", "dom"), None, None),
        P(("grp", "dom"), None),
        P(("grp", "dom")),
        P(("grp", "dom")),
        P(("grp", "dom")),
        P(("grp", "dom")),
        P(("grp", "dom"), None),
        P(("grp", "dom"), None),
        P(("grp", "dom")),
        P(("grp", "dom")),
    )
    return jax.shard_map(
        per_device,
        mesh=mesh,
        in_specs=placed,
        out_specs=(P("grp", None), P("grp", None)),
        check_vma=False,
    )
```

```python
import jax
import jax.numpy as jnp
from jax import lax
from jax.sharding import PartitionSpec as P
from jax.experimental import pallas as pl
from jax.experimental.pallas import tpu as pltpu

CROSS_CAP = 3


def corner_table(var_count):
    nodes = -1.0 + 2.0 * jnp.arange(4, dtype=jnp.float32) / 3.0
    basis = jnp.stack(((1.0 - nodes) / 2.0, (1.0 + nodes) / 2.0), axis=1)
    cube = jnp.einsum("ia,jb,kc->abcijk", basis, basis, basis).reshape(8, 64)
    return jnp.kron(jnp.eye(var_count, dtype=jnp.float32), cube)


def restrictor(weights, orient):
    var_count = weights.shape[1] // 64
    table = corner_table(var_count)
    full = weights[:, None, :] * table[None]
    shaped = full.reshape(weights.shape[0], var_count * 8, var_count, 4, 4, 4)
    bits = orient.reshape(-1, 1, 1, 1, 1, 1)
    shaped = jnp.where(bits % 2 == 1, jnp.flip(shaped, 3), shaped)
    shaped = jnp.where(bits // 2 % 2 == 1, jnp.flip(shaped, 4), shaped)
    shaped = jnp.where(bits // 4 % 2 == 1, jnp.flip(shaped, 5), shaped)
    return shaped.reshape(weights.shape[0], var_count * 8, var_count * 64).astype(jnp.bfloat16)


def plain_restrictor(weights):
    table = corner_table(weights.shape[1] // 64)
    return (weights[:, None, :] * table[None]).astype(jnp.bfloat16)


def pick_rows(index, table):
    picks = (index[:, None] == jnp.arange(table.shape[0], dtype=jnp.int32)[None, :]).astype(
        jnp.float32
    )
    return jnp.dot(picks, table, precision=lax.Precision.HIGHEST)


def one_sided(blocks, column_side):
    return jnp.einsum(
        "rcj,rij->rci", column_side, blocks, preferred_element_type=jnp.float32
    ).astype(jnp.bfloat16)


def coarse_terms(row_side, products):
    return jnp.einsum("rci,rdi->rcd", row_side, products, preferred_element_type=jnp.float32)


def direct_gather(xs, axes, order, collective_id):
    sizes = [lax.axis_size(axis) for axis in axes]

    def device(axis, peer):
        return tuple(peer if name == axis else lax.axis_index(name) for name in order)

    def kernel(*refs):
        x_refs = refs[: len(axes)]
        outs = refs[len(axes) : 2 * len(axes)]
        send_sem, recv_sem, local_sem = refs[2 * len(axes) :]
        barrier = pltpu.get_barrier_semaphore()
        for axis, n in zip(axes, sizes):
            me = lax.axis_index(axis)
            for step in range(1, n):
                pl.semaphore_signal(
                    barrier, 1, device_id=device(axis, lax.rem(me + step, n)),
                    device_id_type=pl.DeviceIdType.MESH,
                )
        pl.semaphore_wait(barrier, sum(n - 1 for n in sizes))
        locals_ = []
        sends = []
        base = 0
        for a, (axis, n) in enumerate(zip(axes, sizes)):
            me = lax.axis_index(axis)
            x_ref = x_refs[a]
            local = pltpu.make_async_copy(x_ref, outs[a].at[me], local_sem.at[a])
            local.start()
            locals_.append(local)
            for step in range(1, n):
                copy = pltpu.make_async_remote_copy(
                    src_ref=x_ref,
                    dst_ref=outs[a].at[me],
                    send_sem=send_sem.at[base + step],
                    recv_sem=recv_sem.at[base + step],
                    device_id=device(axis, lax.rem(me + step, n)),
                    device_id_type=pl.DeviceIdType.MESH,
                )
                copy.start()
                sends.append(copy)
            base += n
        for copy in sends:
            copy.wait_send()
        base = 0
        for a, (axis, n) in enumerate(zip(axes, sizes)):
            me = lax.axis_index(axis)
            for step in range(1, n):
                source = lax.rem(me - step + n, n)
                pltpu.make_async_remote_copy(
                    src_ref=x_refs[a],
                    dst_ref=outs[a].at[source],
                    send_sem=send_sem.at[base + step],
                    recv_sem=recv_sem.at[base + step],
                    device_id=device(axis, source),
                    device_id_type=pl.DeviceIdType.MESH,
                ).wait_recv()
            base += n
        for local in locals_:
            local.wait()

    total = sum(sizes)
    return pl.pallas_call(
        kernel,
        out_shape=tuple(
            jax.ShapeDtypeStruct((n,) + x.shape, x.dtype) for n, x in zip(sizes, xs)
        ),
        in_specs=[pl.BlockSpec(memory_space=pl.ANY) for _ in sizes],
        out_specs=tuple(pl.BlockSpec(memory_space=pl.ANY) for _ in sizes),
        scratch_shapes=[
            pltpu.SemaphoreType.DMA((total,)),
            pltpu.SemaphoreType.DMA((total,)),
            pltpu.SemaphoreType.DMA((len(axes),)),
        ],
        compiler_params=pltpu.CompilerParams(
            collective_id=collective_id, has_side_effects=True
        ),
    )(*xs)


def id_row(values, width):
    flat = values.reshape(-1).astype(jnp.bfloat16)
    return jnp.pad(flat, (0, width - flat.shape[0]))[None, :]


def per_device(
    diag_blocks,
    face_in,
    face_cross,
    metric,
    source_in,
    source_cross,
    orient_in,
    orient_cross,
    peer_in,
    peer_cross,
    target_in,
    target_cross,
):
    elem_count = metric.shape[0]
    coarse_width = metric.shape[1] // 8
    square = coarse_width * coarse_width
    slots_dev = 3 * elem_count
    group_width = lax.axis_size("dom")
    group_count = lax.axis_size("grp")
    my_dom = lax.axis_index("dom")
    my_grp = lax.axis_index("grp")
    inner_count = face_in.shape[0]
    cross_count = face_cross.shape[0]

    order = ("grp", "dom")
    peer_x = peer_cross[:, 0]
    peer_i = peer_in[:, 0]
    id_cols = jnp.zeros((elem_count, 128), jnp.float32)
    id_cols = id_cols.at[:cross_count, 0].set(peer_x.astype(jnp.float32))
    id_cols = id_cols.at[:cross_count, 1].set(target_cross.astype(jnp.float32))
    metric_ids = jnp.concatenate((metric, id_cols), axis=1)
    fine = metric.shape[1]
    dom_got, grp_got = direct_gather((metric, metric_ids), ("dom", "grp"), order, 0)
    metric_dom = dom_got[:, :, :fine].reshape(-1, fine)
    metric_grp = grp_got[:, :, :fine].reshape(-1, fine)
    got_peer = grp_got[:, :cross_count, fine].astype(jnp.int32)
    got_target = grp_got[:, :cross_count, fine + 1].astype(jnp.int32)

    match = got_peer == my_grp
    rank = jnp.cumsum(match.astype(jnp.int32), axis=1) - 1
    picks = match[:, None, :] & (
        rank[:, None, :] == jnp.arange(CROSS_CAP, dtype=jnp.int32)[None, :, None]
    )
    mine_target = jnp.sum(jnp.where(picks, got_target[:, None, :], 0), axis=2)
    mine_slot = jnp.where(
        jnp.any(picks, axis=2), my_dom * slots_dev + mine_target, -1
    ).reshape(-1)
    inner_slot = peer_i * slots_dev + target_in
    slots = jnp.concatenate((inner_slot, mine_slot), axis=0)
    valid = slots >= 0
    slot_code = jnp.stack(
        (jnp.where(valid, slots // 32, -1), jnp.where(valid, slots % 32, 0)), axis=1
    )

    diag_side = plain_restrictor(metric)
    diag_c = coarse_terms(diag_side, one_sided(diag_blocks, diag_side))
    diag_rows = diag_c.reshape(elem_count, square).astype(jnp.bfloat16)
    diag_all = lax.all_gather(diag_rows, "dom", axis=0)

    cross_y = one_sided(face_cross, restrictor(pick_rows(source_cross, metric), orient_cross))
    cross_row_side = plain_restrictor(
        pick_rows(peer_x * elem_count + target_cross // 3, metric_grp)
    )
    cross_c = coarse_terms(cross_row_side, cross_y).reshape(cross_count, square)
    (got_rows,) = direct_gather((cross_c.astype(jnp.bfloat16),), ("grp",), order, 1)
    mine_rows = jnp.einsum(
        "skr,srq->skq", picks.astype(jnp.bfloat16), got_rows, preferred_element_type=jnp.float32
    ).astype(jnp.bfloat16).reshape(group_count * CROSS_CAP, square)

    inner_y = one_sided(face_in, restrictor(pick_rows(source_in, metric), orient_in))
    inner_row_side = plain_restrictor(
        pick_rows(peer_i * elem_count + target_in // 3, metric_dom)
    )
    inner_c = coarse_terms(inner_row_side, inner_y).reshape(inner_count, square)

    face_packet = jnp.concatenate(
        (inner_c.astype(jnp.bfloat16), id_row(slot_code, square)), axis=0
    )
    face_all = lax.all_gather(face_packet, "dom", axis=0)
    (cross_all,) = direct_gather((mine_rows,), ("dom",), order, 2)
    contrib_count = slots.shape[0]
    codes = face_all[:, inner_count, : 2 * contrib_count].astype(jnp.int32)
    got_slot = jnp.where(codes[:, 0::2] >= 0, codes[:, 0::2] * 32 + codes[:, 1::2], -1)
    inner_got = jnp.pad(got_slot[:, :inner_count], ((0, 0), (0, 1)), constant_values=-1)
    cross_got = got_slot[:, inner_count:]
    group_elems = group_width * elem_count
    faces = []
    for slot in range(3):
        wanted = (jnp.arange(group_elems, dtype=jnp.int32) * 3 + slot)[:, None, None]
        from_inner = jnp.einsum(
            "sdr,drq->sq", (wanted == inner_got[None]).astype(jnp.bfloat16), face_all,
            preferred_element_type=jnp.float32,
        )
        from_cross = jnp.einsum(
            "sdr,drq->sq", (wanted == cross_got[None]).astype(jnp.bfloat16), cross_all,
            preferred_element_type=jnp.float32,
        )
        faces.append(from_inner + from_cross)
    face = jnp.concatenate(faces, axis=1)

    coarse_diag = diag_all[:, :elem_count, :].reshape(-1, square).astype(jnp.float32)
    coarse_face = face.reshape(group_width * elem_count, 3 * square)
    return (coarse_diag, coarse_face)


def solution(mesh):
    placed = (
        P(("grp", "dom"), None, None),
        P(("grp", "dom"), None, None),
        P(("grp", "dom"), None, None),
        P(("grp", "dom"), None),
        P(("grp", "dom")),
        P(("grp", "dom")),
        P(("grp", "dom")),
        P(("grp", "dom")),
        P(("grp", "dom"), None),
        P(("grp", "dom"), None),
        P(("grp", "dom")),
        P(("grp", "dom")),
    )
    return jax.shard_map(
        per_device,
        mesh=mesh,
        in_specs=placed,
        out_specs=(P("grp", None), P("grp", None)),
        check_vma=False,
    )
```

```python
import jax
import jax.numpy as jnp
from jax import lax
from jax.sharding import PartitionSpec as P
from jax.experimental import pallas as pl
from jax.experimental.pallas import tpu as pltpu

CROSS_CAP = 3


def corner_table(var_count):
    nodes = -1.0 + 2.0 * jnp.arange(4, dtype=jnp.float32) / 3.0
    basis = jnp.stack(((1.0 - nodes) / 2.0, (1.0 + nodes) / 2.0), axis=1)
    cube = jnp.einsum("ia,jb,kc->abcijk", basis, basis, basis).reshape(8, 64)
    return jnp.kron(jnp.eye(var_count, dtype=jnp.float32), cube)


def restrictor(weights, orient):
    var_count = weights.shape[1] // 64
    table = corner_table(var_count)
    full = weights[:, None, :] * table[None]
    shaped = full.reshape(weights.shape[0], var_count * 8, var_count, 4, 4, 4)
    bits = orient.reshape(-1, 1, 1, 1, 1, 1)
    shaped = jnp.where(bits % 2 == 1, jnp.flip(shaped, 3), shaped)
    shaped = jnp.where(bits // 2 % 2 == 1, jnp.flip(shaped, 4), shaped)
    shaped = jnp.where(bits // 4 % 2 == 1, jnp.flip(shaped, 5), shaped)
    return shaped.reshape(weights.shape[0], var_count * 8, var_count * 64).astype(jnp.bfloat16)


def plain_restrictor(weights):
    table = corner_table(weights.shape[1] // 64)
    return (weights[:, None, :] * table[None]).astype(jnp.bfloat16)


def pick_rows(index, table):
    picks = (index[:, None] == jnp.arange(table.shape[0], dtype=jnp.int32)[None, :]).astype(
        jnp.float32
    )
    return jnp.dot(picks, table, precision=lax.Precision.HIGHEST)


def one_sided(blocks, column_side):
    return jnp.einsum(
        "rcj,rij->rci", column_side, blocks, preferred_element_type=jnp.float32
    ).astype(jnp.bfloat16)


def coarse_terms(row_side, products):
    return jnp.einsum("rci,rdi->rcd", row_side, products, preferred_element_type=jnp.float32)


def direct_gather(xs, axes, order, collective_id):
    sizes = [lax.axis_size(axis) for axis in axes]

    def device(axis, peer):
        return tuple(peer if name == axis else lax.axis_index(name) for name in order)

    def kernel(*refs):
        x_refs = refs[: len(axes)]
        outs = refs[len(axes) : 2 * len(axes)]
        send_sem, recv_sem, local_sem = refs[2 * len(axes) :]
        barrier = pltpu.get_barrier_semaphore()
        for axis, n in zip(axes, sizes):
            me = lax.axis_index(axis)
            for step in range(1, n):
                pl.semaphore_signal(
                    barrier, 1, device_id=device(axis, lax.rem(me + step, n)),
                    device_id_type=pl.DeviceIdType.MESH,
                )
        pl.semaphore_wait(barrier, sum(n - 1 for n in sizes))
        locals_ = []
        sends = []
        base = 0
        for a, (axis, n) in enumerate(zip(axes, sizes)):
            me = lax.axis_index(axis)
            x_ref = x_refs[a]
            local = pltpu.make_async_copy(x_ref, outs[a].at[me], local_sem.at[a])
            local.start()
            locals_.append(local)
            for step in range(1, n):
                copy = pltpu.make_async_remote_copy(
                    src_ref=x_ref,
                    dst_ref=outs[a].at[me],
                    send_sem=send_sem.at[base + step],
                    recv_sem=recv_sem.at[base + step],
                    device_id=device(axis, lax.rem(me + step, n)),
                    device_id_type=pl.DeviceIdType.MESH,
                )
                copy.start()
                sends.append(copy)
            base += n
        for copy in sends:
            copy.wait_send()
        base = 0
        for a, (axis, n) in enumerate(zip(axes, sizes)):
            me = lax.axis_index(axis)
            for step in range(1, n):
                source = lax.rem(me - step + n, n)
                pltpu.make_async_remote_copy(
                    src_ref=x_refs[a],
                    dst_ref=outs[a].at[source],
                    send_sem=send_sem.at[base + step],
                    recv_sem=recv_sem.at[base + step],
                    device_id=device(axis, source),
                    device_id_type=pl.DeviceIdType.MESH,
                ).wait_recv()
            base += n
        for local in locals_:
            local.wait()

    total = sum(sizes)
    return pl.pallas_call(
        kernel,
        out_shape=tuple(
            jax.ShapeDtypeStruct((n,) + x.shape, x.dtype) for n, x in zip(sizes, xs)
        ),
        in_specs=[pl.BlockSpec(memory_space=pl.ANY) for _ in sizes],
        out_specs=tuple(pl.BlockSpec(memory_space=pl.ANY) for _ in sizes),
        scratch_shapes=[
            pltpu.SemaphoreType.DMA((total,)),
            pltpu.SemaphoreType.DMA((total,)),
            pltpu.SemaphoreType.DMA((len(axes),)),
        ],
        compiler_params=pltpu.CompilerParams(
            collective_id=collective_id, has_side_effects=True
        ),
    )(*xs)


def slot_codes(slots):
    valid = slots >= 0
    return jnp.stack((jnp.where(valid, slots // 32, -1), jnp.where(valid, slots % 32, 0)), axis=1)


def read_codes(row, count):
    codes = row[:, : 2 * count].astype(jnp.int32)
    return jnp.where(codes[:, 0::2] >= 0, codes[:, 0::2] * 32 + codes[:, 1::2], -1)


def id_row(values, width):
    flat = values.reshape(-1).astype(jnp.bfloat16)
    return jnp.pad(flat, (0, width - flat.shape[0]))[None, :]


def device_body(
    diag_blocks,
    face_in,
    face_cross,
    metric,
    source_in,
    source_cross,
    orient_in,
    orient_cross,
    peer_in,
    peer_cross,
    target_in,
    target_cross,
):
    elem_count = metric.shape[0]
    coarse_width = metric.shape[1] // 8
    square = coarse_width * coarse_width
    slots_dev = 3 * elem_count
    group_width = lax.axis_size("dom")
    group_count = lax.axis_size("grp")
    my_dom = lax.axis_index("dom")
    my_grp = lax.axis_index("grp")
    inner_count = face_in.shape[0]
    cross_count = face_cross.shape[0]

    order = ("grp", "dom")
    peer_x = peer_cross[:, 0]
    peer_i = peer_in[:, 0]
    id_cols = jnp.zeros((elem_count, 128), jnp.float32)
    id_cols = id_cols.at[:cross_count, 0].set(peer_x.astype(jnp.float32))
    id_cols = id_cols.at[:cross_count, 1].set(target_cross.astype(jnp.float32))
    metric_ids = jnp.concatenate((metric, id_cols), axis=1)
    fine = metric.shape[1]
    dom_got, grp_got = direct_gather((metric, metric_ids), ("dom", "grp"), order, 0)
    metric_dom = dom_got[:, :, :fine].reshape(-1, fine)
    metric_grp = grp_got[:, :, :fine].reshape(-1, fine)
    got_peer = grp_got[:, :cross_count, fine].astype(jnp.int32)
    got_target = grp_got[:, :cross_count, fine + 1].astype(jnp.int32)

    match = got_peer == my_grp
    rank = jnp.cumsum(match.astype(jnp.int32), axis=1) - 1
    picks = match[:, None, :] & (
        rank[:, None, :] == jnp.arange(CROSS_CAP, dtype=jnp.int32)[None, :, None]
    )
    mine_target = jnp.sum(jnp.where(picks, got_target[:, None, :], 0), axis=2)
    mine_slot = jnp.where(
        jnp.any(picks, axis=2), my_dom * slots_dev + mine_target, -1
    ).reshape(-1)
    inner_slot = peer_i * slots_dev + target_in

    diag_side = plain_restrictor(metric)
    diag_c = coarse_terms(diag_side, one_sided(diag_blocks, diag_side))
    diag_rows = diag_c.reshape(elem_count, square).astype(jnp.bfloat16)
    diag_all = lax.all_gather(diag_rows, "dom", axis=0)

    cross_y = one_sided(face_cross, restrictor(pick_rows(source_cross, metric), orient_cross))
    cross_row_side = plain_restrictor(
        pick_rows(peer_x * elem_count + target_cross // 3, metric_grp)
    )
    cross_c = coarse_terms(cross_row_side, cross_y).reshape(cross_count, square)
    (got_rows,) = direct_gather((cross_c.astype(jnp.bfloat16),), ("grp",), order, 1)
    mine_rows = jnp.einsum(
        "skr,srq->skq", picks.astype(jnp.bfloat16), got_rows, preferred_element_type=jnp.float32
    ).astype(jnp.bfloat16).reshape(group_count * CROSS_CAP, square)

    inner_y = one_sided(face_in, restrictor(pick_rows(source_in, metric), orient_in))
    inner_row_side = plain_restrictor(
        pick_rows(peer_i * elem_count + target_in // 3, metric_dom)
    )
    inner_c = coarse_terms(inner_row_side, inner_y).reshape(inner_count, square)

    face_packet = jnp.concatenate(
        (inner_c.astype(jnp.bfloat16), id_row(slot_codes(inner_slot), square)), axis=0
    )
    face_all = lax.all_gather(face_packet, "dom", axis=0)
    cross_packet = jnp.concatenate((mine_rows, id_row(slot_codes(mine_slot), square)), axis=0)
    (cross_all,) = direct_gather((cross_packet,), ("dom",), order, 2)
    inner_got = jnp.pad(
        read_codes(face_all[:, inner_count], inner_count), ((0, 0), (0, 1)), constant_values=-1
    )
    cross_got = jnp.pad(
        read_codes(cross_all[:, mine_rows.shape[0]], mine_rows.shape[0]),
        ((0, 0), (0, 1)), constant_values=-1,
    )
    group_elems = group_width * elem_count
    faces = []
    for slot in range(3):
        wanted = (jnp.arange(group_elems, dtype=jnp.int32) * 3 + slot)[:, None, None]
        from_inner = jnp.einsum(
            "sdr,drq->sq", (wanted == inner_got[None]).astype(jnp.bfloat16), face_all,
            preferred_element_type=jnp.float32,
        )
        from_cross = jnp.einsum(
            "sdr,drq->sq", (wanted == cross_got[None]).astype(jnp.bfloat16), cross_all,
            preferred_element_type=jnp.float32,
        )
        faces.append(from_inner + from_cross)
    face = jnp.concatenate(faces, axis=1)

    coarse_diag = diag_all[:, :elem_count, :].reshape(-1, square).astype(jnp.float32)
    coarse_face = face.reshape(group_width * elem_count, 3 * square)
    return (coarse_diag, coarse_face)


def solution(mesh):
    placed = (
        P(("grp", "dom"), None, None),
        P(("grp", "dom"), None, None),
        P(("grp", "dom"), None, None),
        P(("grp", "dom"), None),
        P(("grp", "dom")),
        P(("grp", "dom")),
        P(("grp", "dom")),
        P(("grp", "dom")),
        P(("grp", "dom"), None),
        P(("grp", "dom"), None),
        P(("grp", "dom")),
        P(("grp", "dom")),
    )
    return jax.shard_map(
        device_body,
        mesh=mesh,
        in_specs=placed,
        out_specs=(P("grp", None), P("grp", None)),
        check_vma=False,
    )
```

```python
import jax
import jax.numpy as jnp
from jax import lax
from jax.sharding import PartitionSpec as P
from jax.experimental import pallas as pl
from jax.experimental.pallas import tpu as pltpu

CROSS_CAP = 3


def corner_table(var_count):
    nodes = -1.0 + 2.0 * jnp.arange(4, dtype=jnp.float32) / 3.0
    basis = jnp.stack(((1.0 - nodes) / 2.0, (1.0 + nodes) / 2.0), axis=1)
    cube = jnp.einsum("ia,jb,kc->abcijk", basis, basis, basis).reshape(8, 64)
    return jnp.kron(jnp.eye(var_count, dtype=jnp.float32), cube)


def restrictor(weights, orient):
    var_count = weights.shape[1] // 64
    table = corner_table(var_count)
    full = weights[:, None, :] * table[None]
    shaped = full.reshape(weights.shape[0], var_count * 8, var_count, 4, 4, 4)
    bits = orient.reshape(-1, 1, 1, 1, 1, 1)
    shaped = jnp.where(bits % 2 == 1, jnp.flip(shaped, 3), shaped)
    shaped = jnp.where(bits // 2 % 2 == 1, jnp.flip(shaped, 4), shaped)
    shaped = jnp.where(bits // 4 % 2 == 1, jnp.flip(shaped, 5), shaped)
    return shaped.reshape(weights.shape[0], var_count * 8, var_count * 64).astype(jnp.bfloat16)


def plain_restrictor(weights):
    table = corner_table(weights.shape[1] // 64)
    return (weights[:, None, :] * table[None]).astype(jnp.bfloat16)


def pick_rows(index, table):
    picks = (index[:, None] == jnp.arange(table.shape[0], dtype=jnp.int32)[None, :]).astype(
        jnp.float32
    )
    return jnp.dot(picks, table, precision=lax.Precision.HIGHEST)


def one_sided(blocks, column_side):
    return jnp.einsum(
        "rcj,rij->rci", column_side, blocks, preferred_element_type=jnp.float32
    ).astype(jnp.bfloat16)


def coarse_terms(row_side, products):
    return jnp.einsum("rci,rdi->rcd", row_side, products, preferred_element_type=jnp.float32)


def direct_gather(xs, axes, order, collective_id):
    sizes = [lax.axis_size(axis) for axis in axes]

    def device(axis, peer):
        return tuple(peer if name == axis else lax.axis_index(name) for name in order)

    def kernel(*refs):
        x_refs = refs[: len(axes)]
        outs = refs[len(axes) : 2 * len(axes)]
        send_sem, recv_sem, local_sem = refs[2 * len(axes) :]
        barrier = pltpu.get_barrier_semaphore()
        for axis, n in zip(axes, sizes):
            me = lax.axis_index(axis)
            for step in range(1, n):
                pl.semaphore_signal(
                    barrier, 1, device_id=device(axis, lax.rem(me + step, n)),
                    device_id_type=pl.DeviceIdType.MESH,
                )
        pl.semaphore_wait(barrier, sum(n - 1 for n in sizes))
        locals_ = []
        sends = []
        base = 0
        for a, (axis, n) in enumerate(zip(axes, sizes)):
            me = lax.axis_index(axis)
            x_ref = x_refs[a]
            local = pltpu.make_async_copy(x_ref, outs[a].at[me], local_sem.at[a])
            local.start()
            locals_.append(local)
            for step in range(1, n):
                copy = pltpu.make_async_remote_copy(
                    src_ref=x_ref,
                    dst_ref=outs[a].at[me],
                    send_sem=send_sem.at[base + step],
                    recv_sem=recv_sem.at[base + step],
                    device_id=device(axis, lax.rem(me + step, n)),
                    device_id_type=pl.DeviceIdType.MESH,
                )
                copy.start()
                sends.append(copy)
            base += n
        for copy in sends:
            copy.wait_send()
        base = 0
        for a, (axis, n) in enumerate(zip(axes, sizes)):
            me = lax.axis_index(axis)
            for step in range(1, n):
                source = lax.rem(me - step + n, n)
                pltpu.make_async_remote_copy(
                    src_ref=x_refs[a],
                    dst_ref=outs[a].at[source],
                    send_sem=send_sem.at[base + step],
                    recv_sem=recv_sem.at[base + step],
                    device_id=device(axis, source),
                    device_id_type=pl.DeviceIdType.MESH,
                ).wait_recv()
            base += n
        for local in locals_:
            local.wait()

    total = sum(sizes)
    return pl.pallas_call(
        kernel,
        out_shape=tuple(
            jax.ShapeDtypeStruct((n,) + x.shape, x.dtype) for n, x in zip(sizes, xs)
        ),
        in_specs=[pl.BlockSpec(memory_space=pl.ANY) for _ in sizes],
        out_specs=tuple(pl.BlockSpec(memory_space=pl.ANY) for _ in sizes),
        scratch_shapes=[
            pltpu.SemaphoreType.DMA((total,)),
            pltpu.SemaphoreType.DMA((total,)),
            pltpu.SemaphoreType.DMA((len(axes),)),
        ],
        compiler_params=pltpu.CompilerParams(
            collective_id=collective_id, has_side_effects=True
        ),
    )(*xs)


def id_row(values, width):
    flat = values.reshape(-1).astype(jnp.bfloat16)
    return jnp.pad(flat, (0, width - flat.shape[0]))[None, :]


def per_device(
    diag_blocks,
    face_in,
    face_cross,
    metric,
    source_in,
    source_cross,
    orient_in,
    orient_cross,
    peer_in,
    peer_cross,
    target_in,
    target_cross,
):
    elem_count = metric.shape[0]
    coarse_width = metric.shape[1] // 8
    square = coarse_width * coarse_width
    slots_dev = 3 * elem_count
    group_width = lax.axis_size("dom")
    group_count = lax.axis_size("grp")
    my_dom = lax.axis_index("dom")
    my_grp = lax.axis_index("grp")
    inner_count = face_in.shape[0]
    cross_count = face_cross.shape[0]

    order = ("grp", "dom")
    peer_x = peer_cross[:, 0]
    peer_i = peer_in[:, 0]
    id_cols = jnp.zeros((elem_count, 128), jnp.float32)
    id_cols = id_cols.at[:cross_count, 0].set(peer_x.astype(jnp.float32))
    id_cols = id_cols.at[:cross_count, 1].set(target_cross.astype(jnp.float32))
    metric_ids = jnp.concatenate((metric, id_cols), axis=1)
    fine = metric.shape[1]
    dom_got, grp_got = direct_gather((metric, metric_ids), ("dom", "grp"), order, 0)
    metric_dom = dom_got[:, :, :fine].reshape(-1, fine)
    metric_grp = grp_got[:, :, :fine].reshape(-1, fine)
    got_peer = grp_got[:, :cross_count, fine].astype(jnp.int32)
    got_target = grp_got[:, :cross_count, fine + 1].astype(jnp.int32)

    match = got_peer == my_grp
    rank = jnp.cumsum(match.astype(jnp.int32), axis=1) - 1
    picks = match[:, None, :] & (
        rank[:, None, :] == jnp.arange(CROSS_CAP, dtype=jnp.int32)[None, :, None]
    )
    mine_target = jnp.sum(jnp.where(picks, got_target[:, None, :], 0), axis=2)
    mine_slot = jnp.where(
        jnp.any(picks, axis=2), my_dom * slots_dev + mine_target, -1
    ).reshape(-1)
    inner_slot = peer_i * slots_dev + target_in
    slots = jnp.concatenate((inner_slot, mine_slot), axis=0)
    valid = slots >= 0
    slot_code = jnp.stack(
        (jnp.where(valid, slots // 32, -1), jnp.where(valid, slots % 32, 0)), axis=1
    )

    diag_side = plain_restrictor(metric)
    diag_c = coarse_terms(diag_side, one_sided(diag_blocks, diag_side))
    diag_rows = diag_c.reshape(elem_count, square).astype(jnp.bfloat16)
    diag_all = lax.all_gather(diag_rows, "dom", axis=0)

    cross_y = one_sided(face_cross, restrictor(pick_rows(source_cross, metric), orient_cross))
    cross_row_side = plain_restrictor(
        pick_rows(peer_x * elem_count + target_cross // 3, metric_grp)
    )
    cross_c = coarse_terms(cross_row_side, cross_y).reshape(cross_count, square)
    (got_rows,) = direct_gather((cross_c.astype(jnp.bfloat16),), ("grp",), order, 1)
    mine_rows = jnp.einsum(
        "skr,srq->skq", picks.astype(jnp.bfloat16), got_rows, preferred_element_type=jnp.float32
    ).astype(jnp.bfloat16).reshape(group_count * CROSS_CAP, square)

    inner_y = one_sided(face_in, restrictor(pick_rows(source_in, metric), orient_in))
    inner_row_side = plain_restrictor(
        pick_rows(peer_i * elem_count + target_in // 3, metric_dom)
    )
    inner_c = coarse_terms(inner_row_side, inner_y).reshape(inner_count, square)

    face_packet = jnp.concatenate(
        (inner_c.astype(jnp.bfloat16), id_row(slot_code, square)), axis=0
    )
    face_all = lax.all_gather(face_packet, "dom", axis=0)
    (cross_all,) = direct_gather((mine_rows,), ("dom",), order, 2)
    contrib_count = slots.shape[0]
    codes = face_all[:, inner_count, : 2 * contrib_count].astype(jnp.int32)
    got_slot = jnp.where(codes[:, 0::2] >= 0, codes[:, 0::2] * 32 + codes[:, 1::2], -1)
    inner_got = jnp.pad(got_slot[:, :inner_count], ((0, 0), (0, 1)), constant_values=-1)
    cross_got = got_slot[:, inner_count:]
    group_elems = group_width * elem_count
    faces = []
    for slot in range(3):
        wanted = (jnp.arange(group_elems, dtype=jnp.int32) * 3 + slot)[:, None, None]
        from_inner = jnp.einsum(
            "sdr,drq->sq", (wanted == inner_got[None]).astype(jnp.bfloat16), face_all,
            preferred_element_type=jnp.float32,
        )
        from_cross = jnp.einsum(
            "sdr,drq->sq", (wanted == cross_got[None]).astype(jnp.bfloat16), cross_all,
            preferred_element_type=jnp.float32,
        )
        faces.append(from_inner + from_cross)
    face = jnp.zeros((group_elems, 3 * square), jnp.float32)
    for slot in range(3):
        face = face.at[:, slot * square : (slot + 1) * square].set(faces[slot])

    coarse_diag = diag_all[:, :elem_count, :].reshape(-1, square).astype(jnp.float32)
    coarse_face = face.reshape(group_width * elem_count, 3 * square)
    return (coarse_diag, coarse_face)


def solution(mesh):
    placed = (
        P(("grp", "dom"), None, None),
        P(("grp", "dom"), None, None),
        P(("grp", "dom"), None, None),
        P(("grp", "dom"), None),
        P(("grp", "dom")),
        P(("grp", "dom")),
        P(("grp", "dom")),
        P(("grp", "dom")),
        P(("grp", "dom"), None),
        P(("grp", "dom"), None),
        P(("grp", "dom")),
        P(("grp", "dom")),
    )
    return jax.shard_map(
        per_device,
        mesh=mesh,
        in_specs=placed,
        out_specs=(P("grp", None), P("grp", None)),
        check_vma=False,
    )
```
